32 devices in a mesh: dp: 16 (over z, y, x), tensor: 2 (over core).
Axes of the slice: x: 2, y: 2, z: 4, core: 2. Of those that a mesh axis runs over, the one named last changes fastest.
Arguments:
- inputs: bfloat16 [25088, 512], P(('dp', 'tensor')), may hold values from -6 to 6
- cotangent: bfloat16 [25088, 512], P(('dp', 'tensor')), may hold values from -6 to 6
- region_ids: int32 [196], replicated, may hold values from 0 to 3
- rel_index: int32 [49, 49], replicated, may hold values from 0 to 168
- norm1_gain: bfloat16 [2, 512], replicated, may hold values from 0.5 to 1.5
- norm1_bias: bfloat16 [2, 512], replicated, may hold values from -1.75 to 1.75
- w_qkv: bfloat16 [2, 3, 512, 512], P(None, None, 'dp', 'tensor'), may hold values from -0.25 to 0.25
- qv_bias: bfloat16 [2, 2, 512], P(None, None, 'tensor'), may hold values from -1.75 to 1.75
- bias_table: bfloat16 [2, 16, 169], P(None, 'tensor'), may hold values from -3 to 250
- w_proj: bfloat16 [2, 512, 512], P(None, 'tensor', 'dp'), may hold values from -0.75 to 0.75
- proj_bias: bfloat16 [2, 512], replicated, may hold values from -1.75 to 1.75
- norm2_gain: bfloat16 [2, 512], replicated, may hold values from 0.5 to 1.5
- norm2_bias: bfloat16 [2, 512], replicated, may hold values from -1.75 to 1.75
- w_fc1: bfloat16 [2, 512, 2048], P(None, 'dp', 'tensor'), may hold values from -0.25 to 0.25
- fc1_bias: bfloat16 [2, 2048], P(None, 'tensor'), may hold values from -3 to 3
- w_fc2: bfloat16 [2, 2048, 512], P(None, 'tensor', 'dp'), may hold values from -0.125 to 0.125
- fc2_bias: bfloat16 [2, 512], replicated, may hold values from -1.75 to 1.75
Outputs:
- outputs: float32 [25088, 512], P(('dp', 'tensor'))
- input_grad: float32 [25088, 512], P(('dp', 'tensor'))
- norm1_gain_grad: float32 [2, 512], replicated
- norm1_bias_grad: float32 [2, 512], replicated
- w_qkv_grad: float32 [2, 3, 512, 512], P(None, None, 'dp', 'tensor')
- qv_bias_grad: float32 [2, 2, 512], P(None, None, 'tensor')
- bias_table_grad: float32 [2, 16, 169], P(None, 'tensor')
- w_proj_grad: float32 [2, 512, 512], P(None, 'tensor', 'dp')
- proj_bias_grad: float32 [2, 512], replicated
- norm2_gain_grad: float32 [2, 512], replicated
- norm2_bias_grad: float32 [2, 512], replicated
- w_fc1_grad: float32 [2, 512, 2048], P(None, 'dp', 'tensor')
- fc1_bias_grad: float32 [2, 2048], P(None, 'tensor')
- w_fc2_grad: float32 [2, 2048, 512], P(None, 'tensor', 'dp')
- fc2_bias_grad: float32 [2, 512], replicated
The draws below stay inside these ranges and needn't reach their ends.
All inputs are finite; a program needn't handle non-finite values.
Results may differ from the reference program's by a relative error of at most 0.025.
Values may be sent and summed in bfloat16 or wider, within the bound.
A program may use at most 192 MiB of HBM per device.

```python
import jax
import jax.numpy as jnp
from jax import lax

C = 512
HEADS = 16
HD = 32
FF = 2048
GRID = 14
WIN = 7
SHIFT = 3
LAYERS = 2
IMG_DEV = 8
TABLE = 169
IMAGES = 128
TOKENS = 25088
N_DP = 16


def draw_bias_table(key, part):
    base_key = jax.random.fold_in(key, 0)
    shape = (LAYERS, HEADS, TABLE)
    values = jnp.clip(jax.random.normal(base_key, shape, jnp.float32), -3.0, 3.0)
    return values.astype(jnp.bfloat16)


def place_ends(values, rng, least, high):
    dims = values.shape
    place = [jax.random.randint(jax.random.fold_in(rng, axis), (), 0, dims[axis]) for axis in range(len(dims))]
    values = values.at[tuple(place)].set(least)
    longest = dims.index(max(dims))
    place[longest] = (place[longest] + 1) % dims[longest]
    return values.at[tuple(place)].set(high)


def levels(own_key, extent, cuts, least, largest):
    def one(dim, parts):
        steps = jax.random.uniform(jax.random.fold_in(jax.random.fold_in(own_key, 6), dim), (parts,), jnp.float32, least / len(cuts), largest / len(cuts))
        return jnp.repeat(jnp.exp(steps), extent[dim] // parts).reshape((-1,) + (1,) * (len(extent) - dim - 1))

    gain = one(*cuts[0])
    for cut in cuts[1:]:
        gain = gain * one(*cut)
    return gain


def normal_values(rng, extent, scale, bound, shards=(), held_as=jnp.bfloat16):
    factor_of = levels(rng, extent, shards, -0.22, 0.18) if shards else 1.0
    entries = jax.random.normal(rng, extent, jnp.float32) * scale * factor_of
    return jnp.minimum(jnp.maximum(entries, -bound), bound).astype(held_as)


def setup_inputs(seed: int = 0) -> dict:
    arg_keys = jax.random.split(jax.random.key(seed), 18)
    inputs = normal_values(arg_keys[0], (TOKENS, C), 1.0, 6.0, ((0, 32),))
    cotangent = normal_values(arg_keys[1], (TOKENS, C), 1.0, 6.0, ((0, 32),))
    region_ids = place_ends(jax.random.randint(arg_keys[2], (GRID * GRID,), 0, 4), jax.random.fold_in(arg_keys[2], 1), 0, 3).astype(jnp.int32)
    rel_index = place_ends(jax.random.randint(arg_keys[3], (WIN * WIN, WIN * WIN), 0, TABLE), jax.random.fold_in(arg_keys[3], 1), 0, TABLE - 1).astype(jnp.int32)
    norm1_gain = jnp.clip(1.0 + 0.1 * jax.random.normal(arg_keys[4], (LAYERS, C), jnp.float32), 0.5, 1.5).astype(jnp.bfloat16)
    norm1_bias = normal_values(arg_keys[5], (LAYERS, C), 0.3, 1.75)
    w_qkv = normal_values(arg_keys[6], (LAYERS, 3, C, C), C ** -0.5, 0.25, ((2, 16), (3, 2)))
    qv_bias = normal_values(arg_keys[7], (LAYERS, 2, C), 0.3, 1.75, ((2, 2),))
    bias_table = draw_bias_table(jax.random.fold_in(arg_keys[17], 71), 0)
    w_proj = normal_values(arg_keys[9], (LAYERS, C, C), (C // WIN) ** -0.5, 0.75, ((1, 2), (2, 16)))
    proj_bias = normal_values(arg_keys[10], (LAYERS, C), 0.3, 1.75)
    norm2_gain = jnp.clip(1.0 + 0.1 * jax.random.normal(arg_keys[11], (LAYERS, C), jnp.float32), 0.5, 1.5).astype(jnp.bfloat16)
    norm2_bias = normal_values(arg_keys[12], (LAYERS, C), 0.3, 1.75)
    w_fc1 = normal_values(arg_keys[13], (LAYERS, C, FF), C ** -0.5, 0.25, ((1, 16), (2, 2)))
    fc1_bias = normal_values(arg_keys[14], (LAYERS, FF), 0.5, 3.0, ((1, 2),))
    w_fc2 = normal_values(arg_keys[15], (LAYERS, FF, C), FF ** -0.5, 0.125, ((1, 2), (2, 16)))
    fc2_bias = normal_values(arg_keys[16], (LAYERS, C), 0.3, 1.75)
    return dict(inputs=inputs, cotangent=cotangent, region_ids=region_ids, rel_index=rel_index, norm1_gain=norm1_gain, norm1_bias=norm1_bias, w_qkv=w_qkv, qv_bias=qv_bias, bias_table=bias_table, w_proj=w_proj, proj_bias=proj_bias, norm2_gain=norm2_gain, norm2_bias=norm2_bias, w_fc1=w_fc1, fc1_bias=fc1_bias, w_fc2=w_fc2, fc2_bias=fc2_bias)


EPS = 1e-05
MASKED = -100.0
EXACT_PRECISION = lax.Precision.HIGHEST

def to_grid(tokens, images):
    per_side = GRID // WIN
    shaped = tokens.reshape(images, per_side, per_side, WIN, WIN, -1)
    return shaped.transpose(0, 1, 3, 2, 4, 5).reshape(images, GRID, GRID, -1)

def to_windows(grid_rows, images):
    per_side = GRID // WIN
    shaped = grid_rows.reshape(images, per_side, WIN, per_side, WIN, -1)
    return shaped.transpose(0, 1, 3, 2, 4, 5).reshape(images * GRID * GRID, -1)

def rolled(tokens, images, offset):
    return to_windows(jnp.roll(to_grid(tokens, images), offset, axis=(1, 2)), images)

def normalize(residual):
    average = lax.optimization_barrier(jnp.mean(residual, -1, keepdims=True))
    centered = residual - average
    inverse = lax.rsqrt(lax.optimization_barrier(jnp.mean(centered * centered, -1, keepdims=True)) + EPS)
    return (centered * inverse, inverse)

def norm_back(grad_out, normed, inverse, gain_value):
    scaled = grad_out * gain_value
    return inverse * (scaled - lax.optimization_barrier(jnp.mean(scaled, -1, keepdims=True)) - normed * lax.optimization_barrier(jnp.mean(scaled * normed, -1, keepdims=True)))

def gelu_parts(hidden_pre):
    cumulative = 0.5 * (1.0 + lax.erf(hidden_pre * 0.7071067811865476))
    density = jnp.exp(-0.5 * hidden_pre * hidden_pre) * 0.3989422804014327
    return (hidden_pre * cumulative, cumulative + hidden_pre * density)

def product(first_operand, second_operand):
    return jnp.dot(first_operand, second_operand, preferred_element_type=jnp.float32)

def exact_einsum(pattern, first_operand, second_operand):
    return jnp.einsum(pattern, first_operand.astype(jnp.float32), second_operand.astype(jnp.float32), precision=EXACT_PRECISION)

def reference(inputs, cotangent, region_ids, rel_index, norm1_gain, norm1_bias, w_qkv, qv_bias, bias_table, w_proj, proj_bias, norm2_gain, norm2_bias, w_fc1, fc1_bias, w_fc2, fc2_bias):
    per_side = GRID // WIN
    windows = per_side * per_side
    win_tokens = WIN * WIN
    score_scale = HD ** (-0.5)
    one_hot = (rel_index[:, :, None] == jnp.arange(TABLE, dtype=jnp.int32)[None, None, :]).astype(jnp.float32)
    regions = region_ids.reshape(windows, win_tokens)
    shift_mask = jnp.where(regions[:, :, None] == regions[:, None, :], 0.0, MASKED).astype(jnp.float32)
    mask_list = [jnp.zeros_like(shift_mask), shift_mask]
    rel_biases = [exact_einsum('ijm,hm->hij', one_hot, bias_table[layer_index]) for layer_index in range(LAYERS)]
    group = IMG_DEV * 4 if N_DP % 4 == 0 else IMG_DEV
    blocks = IMAGES // group
    block_rows = group * GRID * GRID
    head_shape = (group, windows, win_tokens, HEADS, HD)

    def scores_of(layer_index, queries, key_rows):
        return exact_einsum('bwihd,bwjhd->bwhij', queries, key_rows) + rel_biases[layer_index][None, None] + mask_list[layer_index % 2][None, :, None]

    def layer_forward(layer_index, residual):
        shifted_layer = layer_index % 2 == 1
        normed_attn, inverse_attn = normalize(residual)
        attn_in = (normed_attn * norm1_gain[layer_index].astype(jnp.float32) + norm1_bias[layer_index].astype(jnp.float32)).astype(jnp.bfloat16)
        if shifted_layer:
            attn_in = rolled(attn_in, group, -SHIFT)
        stacked_qkv = w_qkv[layer_index]
        query_pre = product(attn_in, stacked_qkv[0]) + qv_bias[layer_index, 0].astype(jnp.float32)
        queries = (query_pre * score_scale).astype(jnp.bfloat16).reshape(head_shape)
        key_rows = product(attn_in, stacked_qkv[1]).astype(jnp.bfloat16).reshape(head_shape)
        values = (product(attn_in, stacked_qkv[2]) + qv_bias[layer_index, 1].astype(jnp.float32)).astype(jnp.bfloat16).reshape(head_shape)
        scores = scores_of(layer_index, queries, key_rows)
        highest = lax.optimization_barrier(jnp.max(scores, -1, keepdims=True))
        exponent = jnp.exp(scores - highest)
        denominator = lax.optimization_barrier(jnp.sum(exponent, -1, keepdims=True))
        attention = exponent / denominator
        log_total = highest + jnp.log(denominator)
        mixture = exact_einsum('bwhij,bwjhd->bwihd', attention.astype(jnp.bfloat16), values).astype(jnp.bfloat16).reshape(block_rows, C)
        projected = product(mixture, w_proj[layer_index])
        if shifted_layer:
            projected = rolled(projected, group, SHIFT)
        residual_mid = residual + projected + proj_bias[layer_index].astype(jnp.float32)
        normed_ffn, inverse_ffn = normalize(residual_mid)
        ffn_in = (normed_ffn * norm2_gain[layer_index].astype(jnp.float32) + norm2_bias[layer_index].astype(jnp.float32)).astype(jnp.bfloat16)
        hidden_pre = product(ffn_in, w_fc1[layer_index]) + fc1_bias[layer_index].astype(jnp.float32)
        activated, gelu_slope = gelu_parts(hidden_pre)
        hidden = activated.astype(jnp.bfloat16)
        residual_out = residual_mid + product(hidden, w_fc2[layer_index]) + fc2_bias[layer_index].astype(jnp.float32)
        stored = (normed_attn, inverse_attn, attn_in, queries, key_rows, values, log_total, mixture, normed_ffn, inverse_ffn, ffn_in, gelu_slope, hidden)
        return (residual_out, stored)

    def layer_backward(layer_index, stored, grad_out):
        shifted_layer = layer_index % 2 == 1
        normed_attn, inverse_attn, attn_in, queries, key_rows, values, log_total, mixture, normed_ffn, inverse_ffn, ffn_in, gelu_slope, hidden = stored
        grad_fc2_bias = lax.optimization_barrier(jnp.sum(grad_out, 0))
        grad_low = grad_out.astype(jnp.bfloat16)
        grad_hidden = product(grad_low, w_fc2[layer_index].T)
        grad_w_fc2 = product(hidden.T, grad_low)
        grad_pre = grad_hidden * gelu_slope
        grad_pre_low = grad_pre.astype(jnp.bfloat16)
        grad_fc1_bias = lax.optimization_barrier(jnp.sum(grad_pre, 0))
        grad_w_fc1 = product(ffn_in.T, grad_pre_low)
        grad_ffn_in = product(grad_pre_low, w_fc1[layer_index].T)
        grad_norm2_gain = lax.optimization_barrier(jnp.sum(grad_ffn_in * normed_ffn, 0))
        grad_norm2_bias = lax.optimization_barrier(jnp.sum(grad_ffn_in, 0))
        grad_mid = grad_out + norm_back(grad_ffn_in, normed_ffn, inverse_ffn, norm2_gain[layer_index].astype(jnp.float32))
        grad_proj_bias = lax.optimization_barrier(jnp.sum(grad_mid, 0))
        grad_mid_low = grad_mid.astype(jnp.bfloat16)
        if shifted_layer:
            grad_mid_low = rolled(grad_mid_low, group, -SHIFT)
        grad_mixture = product(grad_mid_low, w_proj[layer_index].T)
        grad_w_proj = product(mixture.T, grad_mid_low)
        grad_mixture_low = grad_mixture.astype(jnp.bfloat16).reshape(head_shape)
        scores = scores_of(layer_index, queries, key_rows)
        attention = jnp.exp(scores - log_total)
        attention_low = attention.astype(jnp.bfloat16)
        grad_values = exact_einsum('bwhij,bwihd->bwjhd', attention_low, grad_mixture_low).reshape(block_rows, C)
        grad_attention = exact_einsum('bwihd,bwjhd->bwhij', grad_mixture_low, values)
        row_inner = lax.optimization_barrier(jnp.sum(attention * grad_attention, -1, keepdims=True))
        grad_scores = attention * (grad_attention - row_inner)
        grad_table = exact_einsum('ijm,hij->hm', one_hot, lax.optimization_barrier(jnp.sum(grad_scores, (0, 1))))
        grad_scores_low = grad_scores.astype(jnp.bfloat16)
        grad_queries = exact_einsum('bwhij,bwjhd->bwihd', grad_scores_low, key_rows).reshape(block_rows, C) * score_scale
        grad_keys = exact_einsum('bwhij,bwihd->bwjhd', grad_scores_low, queries).reshape(block_rows, C)
        grad_qv_bias = jnp.stack([lax.optimization_barrier(jnp.sum(grad_queries, 0)), lax.optimization_barrier(jnp.sum(grad_values, 0))])
        grad_parts = [grad_queries.astype(jnp.bfloat16), grad_keys.astype(jnp.bfloat16), grad_values.astype(jnp.bfloat16)]
        stacked_qkv = w_qkv[layer_index]
        grad_attn_in = product(grad_parts[0], stacked_qkv[0].T) + product(grad_parts[1], stacked_qkv[1].T) + product(grad_parts[2], stacked_qkv[2].T)
        grad_w_qkv = jnp.stack([product(attn_in.T, grad_part) for grad_part in grad_parts])
        if shifted_layer:
            grad_attn_in = rolled(grad_attn_in, group, SHIFT)
        grad_norm1_gain = lax.optimization_barrier(jnp.sum(grad_attn_in * normed_attn, 0))
        grad_norm1_bias = lax.optimization_barrier(jnp.sum(grad_attn_in, 0))
        grad_in = grad_mid + norm_back(grad_attn_in, normed_attn, inverse_attn, norm1_gain[layer_index].astype(jnp.float32))
        return (grad_in, (grad_norm1_gain, grad_norm1_bias, grad_w_qkv, grad_qv_bias, grad_table, grad_w_proj, grad_proj_bias, grad_norm2_gain, grad_norm2_bias, grad_w_fc1, grad_fc1_bias, grad_w_fc2, grad_fc2_bias))

    def one_block(running_grads, pieces):
        block_in, block_cot = pieces
        residual = block_in.astype(jnp.float32)
        forward_store = []
        for layer_index in range(LAYERS):
            residual, stored = layer_forward(layer_index, residual)
            forward_store.append(stored)
        grad_residual = block_cot.astype(jnp.float32)
        layer_grads = [None] * LAYERS
        for layer_index in reversed(range(LAYERS)):
            grad_residual, layer_grads[layer_index] = layer_backward(layer_index, forward_store[layer_index], grad_residual)
        stacked = tuple((jnp.stack([layer_grads[layer_index][position] for layer_index in range(LAYERS)]) for position in range(13)))
        return (tuple((running + addend for running, addend in zip(running_grads, stacked))), (residual, grad_residual))
    params = (norm1_gain, norm1_bias, w_qkv, qv_bias, bias_table, w_proj, proj_bias, norm2_gain, norm2_bias, w_fc1, fc1_bias, w_fc2, fc2_bias)
    zero_grads = tuple((jnp.zeros(param.shape, jnp.float32) for param in params))
    totals, (block_outs, block_grads) = lax.scan(one_block, zero_grads, (inputs.reshape(blocks, block_rows, C), cotangent.reshape(blocks, block_rows, C)))
    return (block_outs.reshape(TOKENS, C), block_grads.reshape(TOKENS, C), totals[0], totals[1], totals[2], totals[3], totals[4], totals[5], totals[6], totals[7], totals[8], totals[9], totals[10], totals[11], totals[12])
```

```python
import functools
import itertools

import jax
import jax.numpy as jnp
from jax import lax
from jax.experimental import pallas as pl
from jax.experimental.pallas import tpu as pltpu
from jax.sharding import PartitionSpec as P

HD = 32
GRID = 14
WIN = 7
SHIFT = 3
LAYERS = 2
TABLE = 169
EPS = 1e-05
MASKED = -100.0
PADDED = -1e30
SLOT = 64
PER_STEP = 2
LANES = 128
EXACT_PRECISION = lax.Precision.HIGHEST
F32 = jnp.float32
BF16 = jnp.bfloat16


def normalize(residual):
    average = jnp.mean(residual, -1, keepdims=True)
    centered = residual - average
    inverse = lax.rsqrt(jnp.mean(centered * centered, -1, keepdims=True) + EPS)
    return (centered * inverse, inverse)


def norm_back(grad_out, normed, inverse, gain_value):
    scaled = grad_out * gain_value
    return inverse * (
        scaled
        - jnp.mean(scaled, -1, keepdims=True)
        - normed * jnp.mean(scaled * normed, -1, keepdims=True)
    )


def gelu_parts(hidden_pre):
    cumulative = 0.5 * (1.0 + lax.erf(hidden_pre * 0.7071067811865476))
    density = jnp.exp(-0.5 * hidden_pre * hidden_pre) * 0.3989422804014327
    return (hidden_pre * cumulative, cumulative + hidden_pre * density)


def dot(a, b, ca=1, cb=0):
    return lax.dot_general(a, b, (((ca,), (cb,)), ((), ())), preferred_element_type=F32)


def stack_heads(block, masks):
    return jnp.concatenate([block * m for m in masks], axis=0)


def merge_heads(stacked, masks):
    total = None
    for h, m in enumerate(masks):
        part = stacked[h * SLOT : (h + 1) * SLOT] * m
        total = part if total is None else total + part
    return total


def head_masks(dtype):
    lane = lax.broadcasted_iota(jnp.int32, (SLOT, LANES), 1)
    return [
        jnp.where((lane >= h * HD) & (lane < (h + 1) * HD), 1.0, 0.0).astype(dtype)
        for h in range(LANES // HD)
    ]


def probabilities(queries_stacked, keys, bias):
    scores = dot(queries_stacked, keys, 1, 1) + bias
    exponent = jnp.exp(scores - jnp.max(scores, -1, keepdims=True))
    return exponent * (1.0 / jnp.sum(exponent, -1, keepdims=True))


def attention_kernel(qkv_ref, bias_ref, mask_ref, out_ref):
    width = out_ref.shape[1]
    low, full = head_masks(BF16), head_masks(F32)
    for g, w in itertools.product(range(width // LANES), range(mask_ref.shape[0])):
        rows = slice(w * SLOT, (w + 1) * SLOT)
        mask = jnp.concatenate([mask_ref[w]] * len(low), axis=0)
        q = qkv_ref[rows, g * LANES : (g + 1) * LANES]
        k = qkv_ref[rows, width + g * LANES : width + (g + 1) * LANES]
        v = qkv_ref[rows, 2 * width + g * LANES : 2 * width + (g + 1) * LANES]
        attention = probabilities(stack_heads(q, low), k, bias_ref[g] + mask)
        mixed = dot(attention.astype(BF16), v)
        out_ref[rows, g * LANES : (g + 1) * LANES] = merge_heads(mixed, full).astype(BF16)


def attention_back_kernel(scale, qkv_ref, dmix_ref, bias_ref, mask_ref, dqkv_ref, dscore_ref, dbias_ref):
    width = dmix_ref.shape[1]
    low, full = head_masks(BF16), head_masks(F32)

    @pl.when(pl.program_id(0) == 0)
    def _():
        dscore_ref[...] = jnp.zeros_like(dscore_ref)
        dbias_ref[...] = jnp.zeros_like(dbias_ref)

    def put(part, g, at_rows, value):
        at = slice(part * width + g * LANES, part * width + (g + 1) * LANES)
        dqkv_ref[at_rows, at] = value.astype(BF16)
        if part != 1:
            rows = value[0:8]
            for r in range(1, SLOT // 8):
                rows = rows + value[r * 8 : (r + 1) * 8]
            dbias_ref[:, at] += rows

    for g, w in itertools.product(range(width // LANES), range(mask_ref.shape[0])):
        rows = slice(w * SLOT, (w + 1) * SLOT)
        mask = jnp.concatenate([mask_ref[w]] * len(low), axis=0)
        q = qkv_ref[rows, g * LANES : (g + 1) * LANES]
        k = qkv_ref[rows, width + g * LANES : width + (g + 1) * LANES]
        v = qkv_ref[rows, 2 * width + g * LANES : 2 * width + (g + 1) * LANES]
        dm = dmix_ref[rows, g * LANES : (g + 1) * LANES]
        q_stacked = stack_heads(q, low)
        dm_stacked = stack_heads(dm, low)
        attention = probabilities(q_stacked, k, bias_ref[g] + mask)
        dattention = dot(dm_stacked, v, 1, 1)
        inner = jnp.sum(attention * dattention, -1, keepdims=True)
        dscores = attention * (dattention - inner)
        dscore_ref[g] += dscores
        dl = dscores.astype(BF16)
        put(0, g, rows, merge_heads(dot(dl, k), full) * scale)
        put(1, g, rows, dot(dl, q_stacked, 0, 0))
        put(2, g, rows, dot(attention.astype(BF16), dm_stacked, 0, 0))


def attention_forward(qkv, bias, mask):
    rows, width = qkv.shape[0], qkv.shape[1] // 3
    windows = mask.shape[0]
    return pl.pallas_call(
        attention_kernel,
        grid=(rows // (PER_STEP * SLOT),),
        out_shape=jax.ShapeDtypeStruct((rows, width), BF16),
        in_specs=[
            pl.BlockSpec((PER_STEP * SLOT, 3 * width), lambda i: (i, 0)),
            pl.BlockSpec(bias.shape, lambda i: (0, 0, 0)),
            pl.BlockSpec((PER_STEP, SLOT, SLOT), lambda i: (lax.rem(i, windows // PER_STEP), 0, 0)),
        ],
        out_specs=pl.BlockSpec((PER_STEP * SLOT, width), lambda i: (i, 0)),
        cost_estimate=pl.CostEstimate(
            flops=rows * width * SLOT * 16, bytes_accessed=rows * width * 8, transcendentals=rows * width * 2
        ),
        name="attention_forward",
    )(qkv, bias, mask)


def attention_backward(qkv, dmix, bias, mask, scale):
    rows, width = dmix.shape
    windows = mask.shape[0]
    return pl.pallas_call(
        functools.partial(attention_back_kernel, scale),
        grid=(rows // (PER_STEP * SLOT),),
        out_shape=(
            jax.ShapeDtypeStruct((rows, 3 * width), BF16),
            jax.ShapeDtypeStruct(bias.shape, F32),
            jax.ShapeDtypeStruct((8, 3 * width), F32),
        ),
        in_specs=[
            pl.BlockSpec((PER_STEP * SLOT, 3 * width), lambda i: (i, 0)),
            pl.BlockSpec((PER_STEP * SLOT, width), lambda i: (i, 0)),
            pl.BlockSpec(bias.shape, lambda i: (0, 0, 0)),
            pl.BlockSpec((PER_STEP, SLOT, SLOT), lambda i: (lax.rem(i, windows // PER_STEP), 0, 0)),
        ],
        out_specs=(
            pl.BlockSpec((PER_STEP * SLOT, 3 * width), lambda i: (i, 0)),
            pl.BlockSpec(bias.shape, lambda i: (0, 0, 0)),
            pl.BlockSpec((8, 3 * width), lambda i: (0, 0)),
        ),
        cost_estimate=pl.CostEstimate(
            flops=rows * width * SLOT * 40, bytes_accessed=rows * width * 16, transcendentals=rows * width * 2
        ),
        name="attention_backward",
    )(qkv, dmix, bias, mask)


def placement(tokens, shift):
    per_side = GRID // WIN
    slots = tokens // (WIN * WIN) * SLOT
    row = lax.broadcasted_iota(jnp.int32, (slots, tokens), 0)
    column = lax.broadcasted_iota(jnp.int32, (slots, tokens), 1)
    window, p = row // SLOT, row % SLOT
    image, w = window // (per_side * per_side), window % (per_side * per_side)
    gi = (w // per_side * WIN + p // WIN + shift) % GRID
    gj = (w % per_side * WIN + p % WIN + shift) % GRID
    source = (
        image * (GRID * GRID)
        + (gi // WIN * per_side + gj // WIN) * (WIN * WIN)
        + gi % WIN * WIN
        + gj % WIN
    )
    return ((column == source) & (p < WIN * WIN)).astype(BF16)


def pack_weights(w_qkv, w_proj, w_fc1, w_fc2):
    rows = w_qkv.shape[1]
    return jnp.concatenate(
        [w_qkv.transpose(1, 0, 2).reshape(rows, -1), w_proj.T, w_fc1, w_fc2.T], axis=1
    )


def per_device(
    inputs,
    cotangent,
    region_ids,
    rel_index,
    norm1_gain,
    norm1_bias,
    w_qkv,
    qv_bias,
    bias_table,
    w_proj,
    proj_bias,
    norm2_gain,
    norm2_bias,
    w_fc1,
    fc1_bias,
    w_fc2,
    fc2_bias,
):
    n_dp, n_t = lax.axis_size("dp"), lax.axis_size("tensor")
    t_index = lax.axis_index("tensor")
    tokens, width = inputs.shape
    ff_local = fc1_bias.shape[1]
    heads_local = bias_table.shape[1]
    heads = heads_local * n_t
    local = heads_local * HD
    shard = width // n_dp
    cuts = (3 * local, 4 * local, 4 * local + ff_local, 4 * local + 2 * ff_local)
    per_side = GRID // WIN
    windows = per_side * per_side
    win_tokens = WIN * WIN
    score_scale = HD ** (-0.5)
    groups = width // LANES

    def pack_grads(g_qkv, g_proj, g_fc1, g_fc2):
        sides = []
        for t in range(n_t):
            pieces = []
            for g, n in ((g_qkv, 3), (g_proj, 1), (g_fc1, 1), (g_fc2, 1)):
                step = g.shape[1] // (n * n_t)
                pieces += [g[:, (m * n_t + t) * step : (m * n_t + t + 1) * step].astype(BF16) for m in range(n)]
            sides.append(jnp.concatenate(pieces, axis=1).reshape(n_dp, shard, -1))
        return jnp.stack(sides, axis=1)

    small = jnp.concatenate([qv_bias.reshape(-1), fc1_bias.reshape(-1), bias_table.reshape(-1)])
    extra = -(-small.shape[0] // (shard * LANES)) * LANES
    small_packed = jnp.pad(small, (0, shard * extra - small.shape[0])).reshape(shard, extra)

    def gather_layer(l):
        packed = pack_weights(w_qkv[l], w_proj[l], w_fc1[l], w_fc2[l])
        if l == 0:
            packed = jnp.concatenate([packed, small_packed], axis=1)
        whole = gather_shards(packed)
        return whole, whole[0, :, :, cuts[3] :].reshape(n_t, -1)

    def unpack_weights(whole):
        blocks = [whole[:, t].reshape(width, -1) for t in range(n_t)]
        parts = []
        lo = 0
        for n, hi in zip((3, 1, 1, 1), cuts):
            step = (hi - lo) // n
            parts.append(
                jnp.concatenate([b[:, lo + m * step : lo + (m + 1) * step] for m in range(n) for b in blocks], axis=1)
            )
            lo = hi
        return parts

    gathered = [gather_layer(l) for l in range(LAYERS)]
    wholes = [whole for whole, _ in gathered]
    weights = [None] * LAYERS
    small = gathered[0][1][:, : small.shape[0]]
    n_qv, n_fc = qv_bias.size, fc1_bias.size
    qv_full = small[:, :n_qv].reshape(n_t, LAYERS, 2, local).transpose(1, 2, 0, 3).reshape(LAYERS, 2, width)
    fc1_full = small[:, n_qv : n_qv + n_fc].reshape(n_t, LAYERS, ff_local).transpose(1, 0, 2).reshape(LAYERS, -1)
    table_full = (
        small[:, n_qv + n_fc :].reshape(n_t, LAYERS, heads_local, TABLE).transpose(1, 0, 2, 3).reshape(LAYERS, heads, TABLE)
    ).astype(F32)
    fc1_full = fc1_full.astype(F32)
    qv_full = qv_full.astype(F32)

    pad = SLOT - win_tokens
    index_padded = jnp.pad(rel_index, ((0, pad), (0, pad)), constant_values=-1).reshape(-1)
    one_hot = (index_padded[None, :] == jnp.arange(TABLE, dtype=jnp.int32)[:, None]).astype(F32)
    regions = region_ids.reshape(windows, win_tokens)
    shift_mask = jnp.where(regions[:, :, None] == regions[:, None, :], 0.0, MASKED).astype(F32)

    def padded_mask(mask):
        return jnp.pad(
            jnp.pad(mask, ((0, 0), (0, pad), (0, 0))), ((0, 0), (0, 0), (0, pad)), constant_values=PADDED
        )

    masks = [padded_mask(jnp.zeros_like(shift_mask)), padded_mask(shift_mask)]
    biases = [
        jnp.dot(table_full[l], one_hot, precision=EXACT_PRECISION).reshape(groups, LANES // HD * SLOT, SLOT)
        for l in range(LAYERS)
    ]
    places = [placement(tokens, SHIFT * (l % 2)) for l in range(LAYERS)]
    scale_row = jnp.concatenate([jnp.full((width,), score_scale, F32), jnp.ones((2 * width,), F32)])

    residual = inputs.astype(F32)
    store = []
    for l in range(LAYERS):
        whole, residual = lax.optimization_barrier((wholes[l], residual)) if l else (wholes[l], residual)
        weights[l] = unpack_weights(whole)
        qkv_w, proj_w, fc1_w, fc2_w = weights[l]
        place = places[l]
        normed1, inverse1 = normalize(residual)
        attn_in = (normed1 * norm1_gain[l].astype(F32) + norm1_bias[l].astype(F32)).astype(BF16)
        attn_pad = dot(place, attn_in).astype(BF16)
        qkv_bias = jnp.concatenate([qv_full[l, 0], jnp.zeros((width,), F32), qv_full[l, 1]])
        qkv = ((dot(attn_pad, qkv_w) + qkv_bias) * scale_row).astype(BF16)
        mixture = dot(place, attention_forward(qkv, biases[l], masks[l % 2]), 0, 0).astype(BF16)
        residual_mid = residual + dot(mixture, proj_w, 1, 1) + proj_bias[l].astype(F32)
        normed2, inverse2 = normalize(residual_mid)
        ffn_in = (normed2 * norm2_gain[l].astype(F32) + norm2_bias[l].astype(F32)).astype(BF16)
        activated, slope = gelu_parts(dot(ffn_in, fc1_w) + fc1_full[l])
        hidden = activated.astype(BF16)
        slope = slope.astype(BF16)
        store.append((normed1, inverse1, attn_in, qkv, mixture, normed2, inverse2, ffn_in, slope, hidden))
        residual = residual_mid + dot(hidden, fc2_w, 1, 1) + fc2_bias[l].astype(F32)

    g = cotangent.astype(F32)
    weight_grads = [None] * LAYERS
    small_grads = [None] * LAYERS
    for l in reversed(range(LAYERS)):
        qkv_w, proj_w, fc1_w, fc2_w = weights[l]
        place = places[l]
        normed1, inverse1, attn_in, qkv, mixture, normed2, inverse2, ffn_in, slope, hidden = store[l]
        g_fc2_bias = jnp.sum(g, 0)
        gl = g.astype(BF16)
        dpre = dot(gl, fc2_w) * slope.astype(F32)
        dpl = dpre.astype(BF16)
        g_fc1_bias = jnp.sum(dpre, 0)
        g_fc2 = dot(gl, hidden, 0, 0)
        g_fc1 = dot(ffn_in, dpl, 0, 0)
        dffn = dot(dpl, fc1_w, 1, 1)
        g_n2_gain = jnp.sum(dffn * normed2, 0)
        g_n2_bias = jnp.sum(dffn, 0)
        g_mid = g + norm_back(dffn, normed2, inverse2, norm2_gain[l].astype(F32))
        g_proj_bias = jnp.sum(g_mid, 0)
        gm = g_mid.astype(BF16)
        g_proj = dot(gm, mixture, 0, 0)
        dmix = dot(gm, proj_w).astype(BF16)
        dmix_pad = dot(place, dmix).astype(BF16)
        dqkv_pad, dscores, dbias = attention_backward(qkv, dmix_pad, biases[l], masks[l % 2], score_scale)
        g_table = lax.dot_general(
            dscores.reshape(heads, SLOT * SLOT), one_hot, (((1,), (1,)), ((), ())), precision=EXACT_PRECISION
        )
        dqkv = dot(place, dqkv_pad, 0, 0).astype(BF16)
        g_qkv = dot(attn_in, dqkv, 0, 0)
        dattn = dot(dqkv, qkv_w, 1, 1)
        g_n1_gain = jnp.sum(dattn * normed1, 0)
        g_n1_bias = jnp.sum(dattn, 0)
        g = g_mid + norm_back(dattn, normed1, inverse1, norm1_gain[l].astype(F32))
        dbias_rows = jnp.sum(dbias, 0)
        weight_grads[l] = reduce_shards(pack_grads(g_qkv, g_proj, g_fc1, g_fc2)).astype(F32)
        small_grads[l] = [
            g_n1_gain, g_n1_bias, g_proj_bias, g_n2_gain, g_n2_bias, g_fc2_bias,
            dbias_rows[:width], dbias_rows[2 * width :], g_fc1_bias, g_table.reshape(-1),
        ]

    flat = jnp.concatenate([v for l in range(LAYERS) for v in small_grads[l]])
    total = sum_everywhere(flat).reshape(LAYERS, -1)
    vectors = total[:, : 6 * width].reshape(LAYERS, 6, width)
    at = 6 * width
    qv_total = total[:, at : at + 2 * width].reshape(LAYERS, 2, width)
    qv_total = lax.dynamic_slice_in_dim(qv_total, t_index * local, local, 2)
    at += 2 * width
    fc1_total = lax.dynamic_slice_in_dim(total[:, at : at + ff_local * n_t], t_index * ff_local, ff_local, 1)
    at += ff_local * n_t
    table_total = lax.dynamic_slice_in_dim(
        total[:, at:].reshape(LAYERS, heads, TABLE), t_index * heads_local, heads_local, 1
    )
    grads = jnp.stack(weight_grads)
    qkv_total = grads[..., : cuts[0]].reshape(LAYERS, shard, 3, local).transpose(0, 2, 1, 3)
    proj_w_total = grads[..., cuts[0] : cuts[1]].transpose(0, 2, 1)
    fc1_w_total = grads[..., cuts[1] : cuts[2]]
    fc2_w_total = grads[..., cuts[2] :].transpose(0, 2, 1)
    return (
        residual,
        g,
        vectors[:, 0],
        vectors[:, 1],
        qkv_total,
        qv_total,
        table_total,
        proj_w_total,
        vectors[:, 2],
        vectors[:, 3],
        vectors[:, 4],
        fc1_w_total,
        fc1_total,
        fc2_w_total,
        vectors[:, 5],
    )


def gather_shards(packed):
    n_dp, n_t = lax.axis_size("dp"), lax.axis_size("tensor")
    rows = lax.all_gather(packed, ("dp", "tensor"), axis=0, tiled=False)
    return rows.reshape((n_dp, n_t) + packed.shape)


def reduce_shards(packed):
    rows = packed.reshape((-1,) + packed.shape[2:])
    return lax.psum_scatter(rows, ("dp", "tensor"), scatter_dimension=0, tiled=False)


def partners():
    found = []
    for axis in ("tensor", "dp"):
        size, bit = lax.axis_size(axis), 1
        assert size & (size - 1) == 0
        me = lax.axis_index(axis)
        while bit < size:
            found.append((axis, me + bit - 2 * bit * ((me // bit) % 2)))
            bit *= 2
    return found


def exchange_kernel(x_ref, out_ref, held, arrived, send_sem, recv_sem):
    steps = partners()
    barrier = pltpu.get_barrier_semaphore()
    for axis, place in steps:
        pl.semaphore_signal(barrier, inc=1, device_id={axis: place}, device_id_type=pl.DeviceIdType.MESH)
    pl.semaphore_wait(barrier, len(steps))
    for s, (axis, place) in enumerate(steps):
        source = x_ref if s == 0 else held.at[s - 1]
        copy = pltpu.make_async_remote_copy(
            src_ref=source,
            dst_ref=arrived.at[s],
            send_sem=send_sem.at[s],
            recv_sem=recv_sem.at[s],
            device_id={axis: place},
            device_id_type=pl.DeviceIdType.MESH,
        )
        copy.start()
        copy.wait()
        total = source[...] + arrived[s]
        if s < len(steps) - 1:
            held[s] = total
        else:
            out_ref[...] = total


def sum_everywhere(flat):
    size = flat.shape[0]
    rows = -(-size // (8 * LANES)) * 8
    x = jnp.pad(flat, (0, rows * LANES - size)).reshape(rows, LANES)
    n = len(partners())
    total = pl.pallas_call(
        exchange_kernel,
        out_shape=jax.ShapeDtypeStruct(x.shape, F32),
        in_specs=[pl.BlockSpec(memory_space=pltpu.VMEM)],
        out_specs=pl.BlockSpec(memory_space=pltpu.VMEM),
        scratch_shapes=[
            pltpu.VMEM((n,) + x.shape, F32),
            pltpu.VMEM((n,) + x.shape, F32),
            pltpu.SemaphoreType.DMA((n,)),
            pltpu.SemaphoreType.DMA((n,)),
        ],
        compiler_params=pltpu.CompilerParams(collective_id=0, has_side_effects=True),
        name="sum_everywhere",
    )(x)
    return total.reshape(-1)[:size]


SMALL_ROWS = 24
TABLE_LANES = 256
PARAMS = ("n1g", "n1b", "pb", "n2g", "n2b", "f2b")


def flip(index, bit):
    return index + bit - 2 * bit * ((index // bit) % 2)


def mix(index, j):
    bit = 1
    while bit <= j:
        if j & bit:
            index = flip(index, bit)
        bit *= 2
    return index


def shift_segments(shift):
    per_side = GRID // WIN
    moves = []
    for w in range(per_side * per_side):
        for p in range(WIN * WIN):
            gi = (w // per_side * WIN + p // WIN + shift) % GRID
            gj = (w % per_side * WIN + p % WIN + shift) % GRID
            source = (gi // WIN * per_side + gj // WIN) * SLOT + gi % WIN * WIN + gj % WIN
            moves.append((w * SLOT + p, source))
    runs = []
    for target, source in moves:
        if runs and runs[-1][0] + runs[-1][2] == target and runs[-1][1] + runs[-1][2] == source:
            runs[-1][2] += 1
        else:
            runs.append([target, source, 1])
    return runs


class Plan:
    def __init__(self, n_dp, tokens, width, ff_local, heads_local):
        self.Y = self.X = 2
        self.Z = n_dp // 4
        self.T = 2
        self.width = width
        self.shard = width // n_dp
        self.local = heads_local * HD
        self.heads_local = heads_local
        self.ffl = ff_local
        self.cols = 4 * self.local + 2 * ff_local
        self.windows = (GRID // WIN) ** 2
        self.images = tokens // (GRID * GRID)
        self.block = self.windows * SLOT
        self.rows = self.images * self.block
        self.groups = self.T * self.local // LANES
        a, b, c = 3 * self.local, 4 * self.local, 4 * self.local + ff_local
        self.at = {"qkv": (0, a), "proj": (a, b), "fc1": (b, c), "fc2": (c, self.cols)}
        self.gather_chunks = [(0, a), (a, c), (c, self.cols)]
        self.scatter_chunks = {"qkv": (0, a), "proj": (a, b), "fc1": (b, c), "fc2": (c, self.cols)}


def halves(cut):
    lo, hi = cut
    step = (hi - lo) // 2 // LANES * LANES
    return ((lo, step), (lo + step, hi - lo - step))


def step_kernel(plan, *refs):
    (x_ref, cot_ref, shard_ref, vec_ref, tab_ref, par_ref, mask_ref, hot_ref,
     out_ref, gin_ref, grad_ref, tot_ref, spill_big, spill_small, spill_inv, spill_qkv,
     W, G1, vecs, tabs, big, low, inv, qkv, gl, mid, bias, dscore, dbias, small, part,
     R0, R1, R2, R3, SR,
     ag_send, ag_recv, rs_send, rs_recv, sm_send, sm_recv, sp_sem) = refs
    Z, T, width, local, ffl = plan.Z, plan.T, plan.width, plan.local, plan.ffl
    block, images, rows = plan.block, plan.images, plan.rows
    L = LAYERS
    dp, t = lax.axis_index("dp"), lax.axis_index("tensor")
    z, y, x = dp // 4, (dp // 2) % 2, dp % 2
    other = 1 - t
    MESH = pl.DeviceIdType.MESH
    to_z = [{"dp": dp + 4 * (mix(z, j) - z)} for j in range(1, Z)]
    to_y, to_x, to_t = {"dp": flip(dp, 2)}, {"dp": flip(dp, 1)}, {"tensor": other}
    pending = []

    def remote(src, dst, send, recv, device):
        return pltpu.make_async_remote_copy(
            src_ref=src, dst_ref=dst, send_sem=send, recv_sem=recv, device_id=device, device_id_type=MESH
        )

    barrier = pltpu.get_barrier_semaphore()
    for device in to_z + [to_y, to_x, to_t]:
        pl.semaphore_signal(barrier, inc=1, device_id=device, device_id_type=MESH)

    xb = [(l, c) for l in range(L) for c in range(len(plan.gather_chunks))]

    def ag_copies(l, c):
        found = []
        for h, (lo, n) in enumerate(halves(plan.gather_chunks[c])):
            k = (l * len(plan.gather_chunks) + c) * 2 + h
            cs = pl.ds(lo, n)
            own = W.at[l, t, z, y, x, :, cs]
            plane = W.at[l, t, :, y, x, :, cs]
            if h == 0:
                wide, new2, new3 = W.at[l, t, :, :, x, :, cs], W.at[l, t, :, 1 - y, x, :, cs], W.at[l, t, :, :, 1 - x, :, cs]
                first, second = to_y, to_x
            else:
                wide, new2, new3 = W.at[l, t, :, y, :, :, cs], W.at[l, t, :, y, 1 - x, :, cs], W.at[l, t, :, 1 - y, :, :, cs]
                first, second = to_x, to_y
            s = lambda i, k=k: (ag_send.at[k, i], ag_recv.at[k, i])
            found.append(dict(
                p1=[remote(shard_ref.at[l, :, cs], own, *s(j), to_z[j]) for j in range(Z - 1)],
                p2=[remote(plane, plane, *s(Z - 1), first)],
                p3=[remote(wide, wide, *s(Z), second)],
                f1=[remote(plane, plane, *s(Z + 1), to_t)],
                f2=[remote(new2, new2, *s(Z + 2), to_t)],
                f3=[remote(new3, new3, *s(Z + 3), to_t)],
            ))
        return found

    def begin(copies):
        for copy in copies:
            copy.start()

    def arrive(copies):
        for copy in copies:
            copy.wait_recv()

    gathers = {key: ag_copies(*key) for key in xb}

    def ag(key, stage):
        for half in gathers[key]:
            if stage == 1:
                begin(half["p1"])
            elif stage == 2:
                arrive(half["p1"])
                begin(half["p2"] + half["f1"])
            elif stage == 3:
                arrive(half["p2"])
                begin(half["p3"] + half["f2"])
            elif stage == 4:
                arrive(half["p3"])
                begin(half["f3"])
            else:
                arrive(half["f1"] + half["f2"] + half["f3"])

    names = ("fc2", "fc1", "proj", "qkv")

    def grads_of(l):
        return G1 if l == L - 1 else W.at[L - 1]

    def rs_copies(l, name):
        found = []
        G = grads_of(l)
        for h, (lo, n) in enumerate(halves(plan.scatter_chunks[name])):
            k = (l * len(names) + names.index(name)) * 2 + h
            cs = pl.ds(lo, n)
            s = lambda i, k=k: (rs_send.at[k, i], rs_recv.at[k, i])
            if h == 0:
                away1, away2, first, second = G.at[t, :, :, 1 - x, :, cs], G.at[t, :, 1 - y, x, :, cs], to_x, to_y
            else:
                away1, away2, first, second = G.at[t, :, 1 - y, :, :, cs], G.at[t, :, y, 1 - x, :, cs], to_y, to_x
            found.append((cs, h, [
                [remote(G.at[other, :, :, :, :, cs], R0.at[l, :, :, :, :, cs], *s(0), to_t)],
                [remote(away1, R1.at[l, :, :, :, cs], *s(1), first)],
                [remote(away2, R2.at[l, :, :, cs], *s(2), second)],
                [remote(G.at[t, mix(z, j), y, x, :, cs], R3.at[l, j - 1, :, cs], *s(2 + j), to_z[j - 1]) for j in range(1, Z)],
            ]))
        return found

    scatters = {(l, name): rs_copies(l, name) for l in range(L) for name in names}

    def plus(a, b):
        return (a.astype(F32) + b.astype(F32)).astype(BF16)

    def rs(key, stage):
        l = key[0]
        G = grads_of(l)
        for cs, h, copies in scatters[key]:
            if stage > 0:
                arrive(copies[stage - 1])
            if stage == 1:
                @pl.loop(0, Z)
                def _(i):
                    G[t, i, :, :, :, cs] = plus(G[t, i, :, :, :, cs], R0[l, i, :, :, :, cs])
            elif stage == 2:
                @pl.loop(0, Z)
                def _(i):
                    for m in range(2):
                        where = (t, i, m, x) if h == 0 else (t, i, y, m)
                        G[(*where, slice(None), cs)] = plus(G[(*where, slice(None), cs)], R1[l, i, m, :, cs])
            elif stage == 3:
                @pl.loop(0, Z)
                def _(i):
                    G[t, i, y, x, :, cs] = plus(G[t, i, y, x, :, cs], R2[l, i, :, cs])
            elif stage == 4:
                total = G[t, z, y, x, :, cs].astype(F32)
                for j in range(1, Z):
                    total = total + R3[l, j - 1, :, cs].astype(F32)
                grad_ref[l, :, cs] = total
            if stage < 4:
                begin(copies[stage])

    def sm_copies():
        s = lambda i: (sm_send.at[i], sm_recv.at[i])
        found = [[remote(part.at[0], SR.at[0], *s(0), to_t)]]
        found.append([remote(part.at[1], SR.at[1], *s(1), to_x)])
        found.append([remote(part.at[2], SR.at[2], *s(2), to_y)])
        found.append([remote(part.at[3], SR.at[2 + j], *s(2 + j), to_z[j - 1]) for j in range(1, Z)])
        return found

    sums = sm_copies()

    def sm(stage):
        if stage > 0:
            arrive(sums[stage - 1])
        if stage == 0:
            part[0] = small[...]
        elif stage < 4:
            part[stage] = part[stage - 1] + SR[stage - 1]
        else:
            level = [part[3]] + [SR[2 + j] for j in range(1, Z)]
            while len(level) > 1:
                level = [level[i] + level[i + 1] for i in range(0, len(level), 2)]
            tot_ref[...] = level[0]
        if stage < 4:
            begin(sums[stage])

    queue = []

    def tick(n=1):
        for _ in range(min(n, len(queue))):
            queue.pop(0)()

    def drain_to(mark):
        while any(getattr(item, "mark", None) == mark for item in queue):
            queue.pop(0)()

    def push(fn, *args, mark=None):
        item = functools.partial(fn, *args)
        item.mark = mark
        queue.append(item)

    def spread(i, count, each=1):
        for k in range(count):
            taken = [queue.pop(0) for _ in range(min(each, len(queue)))]
            if taken:
                @pl.when(i == k)
                def _(taken=taken):
                    for item in taken:
                        item()

    def weight(l, tt, name, lo=None, n=None):
        a, b = plan.at[name]
        value = W[l, tt, :, :, :, :, a:b]
        return value.reshape(width, b - a)

    def put_grad(l, tt, name, first, value):
        a, b = plan.at[name]
        zs = value.shape[0] // (4 * plan.shard)
        grads_of(l)[tt, pl.ds(first, zs), :, :, :, a:b] = value.astype(BF16).reshape(zs, 2, 2, plan.shard, b - a)

    def row_slice(i):
        return pl.ds(pl.multiple_of(i * block, block), block)

    def param(l, name):
        return par_ref[l, PARAMS.index(name)][None, :]

    def add_small(l, row, value, lanes=slice(0, width)):
        small[l, row : row + 1, lanes] += jnp.sum(value, 0, keepdims=True)

    def permute(target, source, shift):
        runs = shift_segments(shift)

        @pl.loop(0, images)
        def _(i):
            base = pl.multiple_of(i * block, block)
            target[pl.ds(base, block), :] = jnp.zeros((block, width), F32)
            src, dst = source.at[pl.ds(base, block)], target.at[pl.ds(base, block)]
            for to, frm, n in runs:
                dst[to : to + n, :] = src[frm : frm + n, :]

    X1, AIN, MIX, X2, FIN = range(5)
    HID, SLOPE = 0, 1
    per = local // LANES

    def group_at(g, part_index):
        return (g // per) * 3 * local + part_index * local + (g % per) * LANES

    scale = HD ** (-0.5)
    low_masks, full_masks = head_masks(BF16), head_masks(F32)

    def win_rows(w):
        return pl.ds(pl.multiple_of(w * SLOT, SLOT), SLOT)

    def load_group(w, g):
        r = win_rows(w)
        return [qkv[r, group_at(g, n) : group_at(g, n) + LANES] for n in range(3)]

    def bias_of(l, w, g):
        per_group = LANES // HD
        mask = mask_ref[l % 2, lax.rem(w, plan.windows)]
        return jnp.concatenate([bias[l, g * per_group + h] + mask for h in range(per_group)], axis=0)

    def forward(l, r):
        @pl.loop(0, images)
        def _(i):
            rs_ = row_slice(i)
            normed, inverse = normalize(r[rs_, :])
            low[X1, rs_, :] = normed.astype(BF16)
            inv[0, rs_, :] = inverse
            low[AIN, rs_, :] = (normed * param(l, "n1g") + param(l, "n1b")).astype(BF16)

        if l == 0:
            drain_to((0, 0))
            prepare()
        else:
            drain_to((l, 0))

        @pl.loop(0, images)
        def _(i):
            rs_ = row_slice(i)
            a = low[AIN, rs_, :]
            for tt in range(T):
                value = dot(a, weight(l, tt, "qkv"))
                at = tt * 3 * local
                qb = vecs[tt, l, 1:2, 0:local]
                vb = vecs[tt, l, 2:3, 0:local]
                qkv[rs_, at : at + local] = ((value[:, :local] + qb) * scale).astype(BF16)
                qkv[rs_, at + local : at + 2 * local] = value[:, local : 2 * local].astype(BF16)
                qkv[rs_, at + 2 * local : at + 3 * local] = (value[:, 2 * local :] + vb).astype(BF16)
            spread(i, images)

        @pl.loop(0, images * plan.windows)
        def _(w):
            for g in range(plan.groups):
                q, k, v = load_group(w, g)
                attention = probabilities(stack_heads(q, low_masks), k, bias_of(l, w, g))
                mixed = dot(attention.astype(BF16), v)
                low[MIX, win_rows(w), g * LANES : (g + 1) * LANES] = merge_heads(mixed, full_masks).astype(BF16)
            spread(w, images * plan.windows)

        drain_to((l, 1))

        @pl.loop(0, images)
        def _(i):
            rs_ = row_slice(i)
            total = r[rs_, :] + param(l, "pb")
            for tt in range(T):
                total = total + dot(low[MIX, rs_, tt * local : (tt + 1) * local], weight(l, tt, "proj"), 1, 1)
            r[rs_, :] = total
            normed, inverse = normalize(total)
            low[X2, rs_, :] = normed.astype(BF16)
            inv[1, rs_, :] = inverse
            low[FIN, rs_, :] = (normed * param(l, "n2g") + param(l, "n2b")).astype(BF16)

        for tt in range(T):
            @pl.loop(0, images)
            def _(i, tt=tt):
                rs_ = row_slice(i)
                pre = dot(low[FIN, rs_, :], weight(l, tt, "fc1")) + vecs[tt, l, 0:1, :]
                activated, slope = gelu_parts(pre)
                big[HID, rs_, tt * ffl : (tt + 1) * ffl] = activated.astype(BF16)
                big[SLOPE, rs_, tt * ffl : (tt + 1) * ffl] = slope.astype(BF16)
                spread(i, images)

        drain_to((l, 2))

        @pl.loop(0, images)
        def _(i):
            rs_ = row_slice(i)
            total = r[rs_, :] + param(l, "f2b")
            for tt in range(T):
                total = total + dot(big[HID, rs_, tt * ffl : (tt + 1) * ffl], weight(l, tt, "fc2"), 1, 1)
            r[rs_, :] = total
            spread(i, images)

    def prepare():
        bias[...] = jnp.zeros_like(bias)
        for tt in range(T):
            @pl.when(t == tt)
            def _(tt=tt):
                vecs[tt] = vec_ref[...]
                tabs[tt] = tab_ref[...]
        arrive(small_in)

        for l in range(L):
            table = jnp.concatenate([tabs[tt, l] for tt in range(T)], axis=0).astype(BF16)

            @pl.loop(0, WIN * WIN)
            def _(i, table=table, l=l):
                line = dot(table, hot_ref[i], 1, 1)
                bias[l, :, pl.ds(i, 1), :] = line[:, None, :]

    def backward(l, g):
        @pl.loop(0, images)
        def _(i):
            rs_ = row_slice(i)
            value = g[rs_, :]
            add_small(l, 5, value)
            gl[rs_, :] = value.astype(BF16)

        half = width // 2
        for tt in range(T):
            fcols = slice(tt * ffl, (tt + 1) * ffl)

            @pl.loop(0, images)
            def _(i, tt=tt, fcols=fcols):
                rs_ = row_slice(i)
                dpre = dot(gl[rs_, :], weight(l, tt, "fc2")) * big[SLOPE, rs_, fcols].astype(F32)
                sums_ = jnp.sum(dpre, 0, keepdims=True)
                for m in range(ffl // width):
                    small[l, 8 + tt * (ffl // width) + m : 9 + tt * (ffl // width) + m, :] += sums_[:, m * width : (m + 1) * width]
                big[SLOPE, rs_, fcols] = dpre.astype(BF16)
                spread(i, images)

            @pl.loop(0, 2)
            def _(m, tt=tt, fcols=fcols):
                lanes = pl.ds(pl.multiple_of(m * half, half), half)
                put_grad(l, tt, "fc2", m * (Z // 2), dot(gl[:, lanes], big[HID, :, fcols], 0, 0))
                spread(m, 2)

        rs((l, "fc2"), 0)
        for tt in range(T):
            fcols = slice(tt * ffl, (tt + 1) * ffl)

            @pl.loop(0, 2)
            def _(m, tt=tt, fcols=fcols):
                lanes = pl.ds(pl.multiple_of(m * half, half), half)
                put_grad(l, tt, "fc1", m * (Z // 2), dot(low[FIN, :, lanes], big[SLOPE, :, fcols], 0, 0))
                spread(m, 2)

        rs((l, "fc1"), 0)
        for stage in range(1, 5):
            push(rs, (l, "fc2"), stage)
            push(rs, (l, "fc1"), stage)

        @pl.loop(0, images)
        def _(i):
            rs_ = row_slice(i)
            dffn = dot(big[SLOPE, rs_, 0:ffl], weight(l, 0, "fc1"), 1, 1)
            for tt in range(1, T):
                dffn = dffn + dot(big[SLOPE, rs_, tt * ffl : (tt + 1) * ffl], weight(l, tt, "fc1"), 1, 1)
            normed = low[X2, rs_, :].astype(F32)
            add_small(l, 3, dffn * normed)
            add_small(l, 4, dffn)
            g_mid = g[rs_, :] + norm_back(dffn, normed, inv[1, rs_, :], param(l, "n2g"))
            add_small(l, 2, g_mid)
            g[rs_, :] = g_mid
            gl[rs_, :] = g_mid.astype(BF16)
            spread(i, images)

        if l > 0:
            fetch("big")
        for tt in range(T):
            @pl.loop(0, 2)
            def _(m, tt=tt):
                lanes = pl.ds(pl.multiple_of(m * half, half), half)
                put_grad(l, tt, "proj", m * (Z // 2), dot(gl[:, lanes], low[MIX, :, tt * local : (tt + 1) * local], 0, 0))
        rs((l, "proj"), 0)
        for stage in range(1, 5):
            push(rs, (l, "proj"), stage)

        @pl.loop(0, images)
        def _(i):
            rs_ = row_slice(i)
            for tt in range(T):
                low[MIX, rs_, tt * local : (tt + 1) * local] = dot(gl[rs_, :], weight(l, tt, "proj")).astype(BF16)

        dscore[...] = jnp.zeros_like(dscore)
        dbias[...] = jnp.zeros_like(dbias)

        @pl.loop(0, images * plan.windows)
        def _(w):
            r = win_rows(w)
            for gg in range(plan.groups):
                q, k, v = load_group(w, gg)
                dm = low[MIX, r, gg * LANES : (gg + 1) * LANES]
                q_stacked, dm_stacked = stack_heads(q, low_masks), stack_heads(dm, low_masks)
                attention = probabilities(q_stacked, k, bias_of(l, w, gg))
                dattention = dot(dm_stacked, v, 1, 1)
                inner = jnp.sum(attention * dattention, -1, keepdims=True)
                dscores = attention * (dattention - inner)
                dscore[pl.ds(gg * 4, 4)] += dscores.reshape(4, SLOT, SLOT)
                dl = dscores.astype(BF16)
                dq = merge_heads(dot(dl, k), full_masks) * scale
                dk = dot(dl, q_stacked, 0, 0)
                dv = dot(attention.astype(BF16), dm_stacked, 0, 0)
                for n, value in enumerate((dq, dk, dv)):
                    qkv[r, group_at(gg, n) : group_at(gg, n) + LANES] = value.astype(BF16)
                    if n != 1:
                        dbias[n // 2, :, gg * LANES : (gg + 1) * LANES] += jnp.sum(value.reshape(SLOT // 8, 8, LANES), 0)
            spread(w, images * plan.windows)

        add_small(l, 6, dbias[0])
        add_small(l, 7, dbias[1])
        if l > 0:
            fetch("mix")
        for tt in range(T):
            at = tt * 3 * local

            @pl.loop(0, 2)
            def _(m, tt=tt, at=at):
                lanes = pl.ds(pl.multiple_of(m * half, half), half)
                put_grad(l, tt, "qkv", m * (Z // 2), dot(low[AIN, :, lanes], qkv[:, at : at + 3 * local], 0, 0))
        rs((l, "qkv"), 0)
        for stage in range(1, 5):
            push(rs, (l, "qkv"), stage)

        @pl.loop(0, images)
        def _(i):
            rs_ = row_slice(i)
            dattn = dot(qkv[rs_, 0 : 3 * local], weight(l, 0, "qkv"), 1, 1)
            for tt in range(1, T):
                dattn = dattn + dot(qkv[rs_, tt * 3 * local : (tt + 1) * 3 * local], weight(l, tt, "qkv"), 1, 1)
            normed = low[X1, rs_, :].astype(F32)
            add_small(l, 0, dattn * normed)
            add_small(l, 1, dattn)
            g[rs_, :] = g[rs_, :] + norm_back(dattn, normed, inv[0, rs_, :], param(l, "n1g"))
            spread(i, images)

        if l > 0:
            fetch("rest")

        n_heads = T * plan.heads_local
        accumulated = jnp.zeros((n_heads, TABLE_LANES), F32)

        def table_step(i, acc):
            line = dscore[:, pl.ds(i, 1), :].reshape(n_heads, SLOT)
            high = line.astype(BF16)
            rest = line - high.astype(F32)
            middle = rest.astype(BF16)
            least = (rest - middle.astype(F32)).astype(BF16)
            three = jnp.concatenate([high, middle, least], axis=0)
            out = dot(three, hot_ref[i])
            return acc + ((out[2 * n_heads :] + out[n_heads : 2 * n_heads]) + out[:n_heads])

        accumulated = lax.fori_loop(0, WIN * WIN, table_step, accumulated)
        hl = n_heads // 2
        small[l, 16 : 16 + hl, 0:TABLE_LANES] = accumulated[:hl]
        small[l, 16 : 16 + hl, TABLE_LANES : 2 * TABLE_LANES] = accumulated[hl:]

    lows = [(low.at[n], spill_small.at[n]) for n in range(5)]
    moves = {
        "ain": [lows[X1], lows[AIN]], "mix": [lows[MIX], lows[X2], lows[FIN]],
        "inv": [(inv, spill_inv)], "qkv": [(qkv, spill_qkv)], "big": [(big, spill_big)],
    }
    order = [pair for name in ("ain", "mix", "inv", "qkv", "big") for pair in moves[name]]
    fetched = []

    def spill():
        copies = [pltpu.make_async_copy(a, b, sp_sem.at[n]) for n, (a, b) in enumerate(order)]
        begin(copies)
        for copy in copies:
            copy.wait()

    def fetch(name):
        which = {
            "big": [7, 3, 4], "mix": [2], "rest": [0, 1, 5, 6],
        }[name]
        for n in which:
            a, b = order[n]
            copy = pltpu.make_async_copy(b, a, sp_sem.at[n])
            copy.start()
            fetched.append(copy)

    def sent(found):
        for copies in found:
            for half in copies:
                for group in half.values():
                    for copy in group:
                        copy.wait_send()

    small_in = [
        remote(vec_ref, vecs.at[t], sm_send.at[2 + Z], sm_recv.at[2 + Z], to_t),
        remote(tab_ref, tabs.at[t], sm_send.at[3 + Z], sm_recv.at[3 + Z], to_t),
    ]
    pl.semaphore_wait(barrier, Z - 1 + 3)
    ag((0, 0), 1)
    begin(small_in)
    for c in range(1, len(plan.gather_chunks)):
        ag((0, c), 1)
    for l in range(L):
        W[l, t, z, y, x] = shard_ref[l]
    small[...] = jnp.zeros_like(small)

    for stage in (2, 3, 4):
        push(ag, (0, 0), stage)
    push(ag, (0, 0), 5, mark=(0, 0))
    push(ag, (0, 1), 2)
    push(ag, (0, 2), 2)
    push(ag, (0, 1), 3)
    for c in range(3):
        push(ag, (1, c), 1)
    push(ag, (0, 2), 3)
    push(ag, (0, 1), 4)
    push(ag, (0, 2), 4)
    push(ag, (0, 1), 5, mark=(0, 1))
    push(ag, (1, 0), 2)
    push(ag, (1, 1), 2)
    push(ag, (0, 2), 5, mark=(0, 2))
    push(ag, (1, 0), 3)
    push(ag, (1, 2), 2)
    push(ag, (1, 1), 3)
    push(ag, (1, 0), 4)
    push(ag, (1, 2), 3)
    push(ag, (1, 1), 4)
    push(ag, (1, 0), 5, mark=(1, 0))
    push(ag, (1, 2), 4)
    push(ag, (1, 1), 5, mark=(1, 1))
    push(ag, (1, 2), 5, mark=(1, 2))

    @pl.loop(0, images)
    def _(i):
        rs_ = row_slice(i)
        out_ref[rs_, :] = x_ref[rs_, :].astype(F32)

    forward(0, out_ref)
    spill()
    permute(mid, out_ref, SHIFT)
    forward(1, mid)
    permute(out_ref, mid, GRID - SHIFT)

    @pl.loop(0, images)
    def _(i):
        rs_ = row_slice(i)
        gin_ref[rs_, :] = cot_ref[rs_, :].astype(F32)

    permute(mid, gin_ref, SHIFT)
    backward(1, mid)
    permute(gin_ref, mid, GRID - SHIFT)
    for copy in fetched:
        copy.wait()
    sent(gathers.values())
    backward(0, gin_ref)
    sm(0)
    tick(1)
    sm(1)
    tick(1)
    sm(2)
    tick(1)
    sm(3)
    tick(1)
    sm(4)
    tick(len(queue))
    for found in scatters.values():
        for _, _, groups in found:
            for group in groups:
                for copy in group:
                    copy.wait_send()
    for group in sums + [small_in]:
        for copy in group:
            copy.wait_send()


def fast_device(
    inputs, cotangent, region_ids, rel_index, norm1_gain, norm1_bias, w_qkv, qv_bias, bias_table, w_proj,
    proj_bias, norm2_gain, norm2_bias, w_fc1, fc1_bias, w_fc2, fc2_bias,
):
    t_index = lax.axis_index("tensor")
    tokens, width = inputs.shape
    plan = Plan(lax.axis_size("dp"), tokens, width, fc1_bias.shape[1], bias_table.shape[1])
    win_tokens = WIN * WIN
    pad = SLOT - win_tokens
    L, T, Z, local, ffl, hl = LAYERS, plan.T, plan.Z, plan.local, plan.ffl, plan.heads_local
    R, C, M = plan.shard, plan.cols, plan.rows

    def padded(array):
        spread_ = array.reshape(tokens // win_tokens, win_tokens, width)
        return jnp.pad(spread_, ((0, 0), (0, pad), (0, 0))).reshape(M, width)

    shards = jnp.stack([pack_weights(w_qkv[l], w_proj[l], w_fc1[l], w_fc2[l]) for l in range(L)])
    vec = jnp.zeros((L, 8, ffl), F32)
    vec = vec.at[:, 0].set(fc1_bias.astype(F32))
    vec = vec.at[:, 1:3, :local].set(qv_bias.astype(F32))
    tab = jnp.pad(bias_table.astype(F32), ((0, 0), (0, 0), (0, TABLE_LANES - TABLE)))
    params = jnp.stack([norm1_gain, norm1_bias, proj_bias, norm2_gain, norm2_bias, fc2_bias], axis=1).astype(F32)
    params = jnp.pad(params, ((0, 0), (0, 2), (0, 0)))
    index_padded = jnp.pad(rel_index, ((0, pad), (0, pad)), constant_values=-1)
    hot = (index_padded[:, :, None] == jnp.arange(TABLE_LANES, dtype=jnp.int32)).astype(BF16)
    regions = region_ids.reshape(plan.windows, win_tokens)
    shift_mask = jnp.where(regions[:, :, None] == regions[:, None, :], 0.0, MASKED).astype(F32)
    mask = jnp.stack([jnp.zeros_like(shift_mask), shift_mask])
    mask = jnp.pad(mask, ((0, 0), (0, 0), (0, pad), (0, 0)))
    mask = jnp.pad(mask, ((0, 0), (0, 0), (0, 0), (0, pad)), constant_values=PADDED)

    vmem = pl.BlockSpec(memory_space=pltpu.VMEM)
    anywhere = pl.BlockSpec(memory_space=pl.ANY)
    n_ag, n_rs = L * 3 * 2, L * 4 * 2
    DMA = pltpu.SemaphoreType.DMA
    outs = pl.pallas_call(
        functools.partial(step_kernel, plan),
        out_shape=(
            jax.ShapeDtypeStruct((M, width), F32),
            jax.ShapeDtypeStruct((M, width), F32),
            jax.ShapeDtypeStruct((L, R, C), F32),
            jax.ShapeDtypeStruct((L, SMALL_ROWS, width), F32),
            jax.ShapeDtypeStruct((2, M, T * ffl), BF16),
            jax.ShapeDtypeStruct((5, M, width), BF16),
            jax.ShapeDtypeStruct((2, M, 1), F32),
            jax.ShapeDtypeStruct((M, 3 * width), BF16),
        ),
        in_specs=[vmem] * 8,
        out_specs=(vmem,) * 4 + (anywhere,) * 4,
        scratch_shapes=[
            pltpu.VMEM((L, T, Z, 2, 2, R, C), BF16),
            pltpu.VMEM((T, Z, 2, 2, R, C), BF16),
            pltpu.VMEM((T, L, 8, ffl), F32),
            pltpu.VMEM((T, L, hl, TABLE_LANES), F32),
            pltpu.VMEM((2, M, T * ffl), BF16),
            pltpu.VMEM((5, M, width), BF16),
            pltpu.VMEM((2, M, 1), F32),
            pltpu.VMEM((M, 3 * width), BF16),
            pltpu.VMEM((M, width), BF16),
            pltpu.VMEM((M, width), F32),
            pltpu.VMEM((L, T * hl, SLOT, SLOT), F32),
            pltpu.VMEM((T * hl, SLOT, SLOT), F32),
            pltpu.VMEM((2, 8, width), F32),
            pltpu.VMEM((L, SMALL_ROWS, width), F32),
            pltpu.VMEM((4, L, SMALL_ROWS, width), F32),
            pltpu.VMEM((L, Z, 2, 2, R, C), BF16),
            pltpu.VMEM((L, Z, 2, R, C), BF16),
            pltpu.VMEM((L, Z, R, C), BF16),
            pltpu.VMEM((L, Z - 1, R, C), BF16),
            pltpu.VMEM((Z + 2, L, SMALL_ROWS, width), F32),
            DMA((n_ag, Z + 4)),
            DMA((n_ag, Z + 4)),
            DMA((n_rs, Z + 2)),
            DMA((n_rs, Z + 2)),
            DMA((Z + 4,)),
            DMA((Z + 4,)),
            DMA((8,)),
        ],
        compiler_params=pltpu.CompilerParams(
            collective_id=0, has_side_effects=True, vmem_limit_bytes=67043328
        ),
        name="whole_step",
    )(padded(inputs), padded(cotangent), shards, vec, tab, params, mask, hot)
    out, g_in, grads, total = outs[:4]

    def unpadded(array):
        return array.reshape(-1, SLOT, width)[:, :win_tokens].reshape(tokens, width)

    qv_total = lax.dynamic_slice_in_dim(total[:, 6:8], t_index * local, local, 2)
    fc1_total = total[:, 8 : 8 + T * ffl // width].reshape(L, T * ffl)
    fc1_total = lax.dynamic_slice_in_dim(fc1_total, t_index * ffl, ffl, 1)
    table_total = lax.dynamic_slice_in_dim(total[:, 16 : 16 + hl], t_index * TABLE_LANES, TABLE_LANES, 2)[..., :TABLE]
    a, b, c = 3 * local, 4 * local, 4 * local + ffl
    return (
        unpadded(out), unpadded(g_in), total[:, 0], total[:, 1],
        grads[..., :a].reshape(L, R, 3, local).transpose(0, 2, 1, 3),
        qv_total, table_total,
        grads[..., a:b].transpose(0, 2, 1),
        total[:, 2], total[:, 3], total[:, 4],
        grads[..., b:c], fc1_total,
        grads[..., c:].transpose(0, 2, 1),
        total[:, 5],
    )


def one_kernel_fits(inputs, bias_table, fc1_bias):
    n_dp, n_t = lax.axis_size("dp"), lax.axis_size("tensor")
    tokens, width = inputs.shape
    z = n_dp // 4
    heads_local = bias_table.shape[1]
    return (
        n_t == 2 and n_dp % 4 == 0 and z >= 2 and z & (z - 1) == 0
        and heads_local * HD % LANES == 0 and heads_local % 8 == 0 and heads_local <= 8
        and width // n_dp % 16 == 0 and width == 2 * TABLE_LANES and fc1_bias.shape[1] % width == 0
        and 8 + 2 * fc1_bias.shape[1] // width <= 16
        and tokens % (GRID * GRID) == 0 and tokens <= 4 * GRID * GRID
    )


def choose(*args):
    if one_kernel_fits(args[0], args[8], args[14]):
        return fast_device(*args)
    return per_device(*args)


def solution(mesh):
    in_specs = (
        P(("dp", "tensor"), None),
        P(("dp", "tensor"), None),
        P(),
        P(),
        P(),
        P(),
        P(None, None, "dp", "tensor"),
        P(None, None, "tensor"),
        P(None, "tensor", None),
        P(None, "tensor", "dp"),
        P(),
        P(),
        P(),
        P(None, "dp", "tensor"),
        P(None, "tensor"),
        P(None, "tensor", "dp"),
        P(),
    )
    out_specs = (
        P(("dp", "tensor"), None),
        P(("dp", "tensor"), None),
        P(),
        P(),
        P(None, None, "dp", "tensor"),
        P(None, None, "tensor"),
        P(None, "tensor", None),
        P(None, "tensor", "dp"),
        P(),
        P(),
        P(),
        P(None, "dp", "tensor"),
        P(None, "tensor"),
        P(None, "tensor", "dp"),
        P(),
    )
    return jax.shard_map(
        choose, mesh=mesh, in_specs=in_specs, out_specs=out_specs, check_vma=False
    )
```

```python
import functools
import itertools

import jax
import jax.numpy as jnp
from jax import lax
from jax.experimental import pallas as pl
from jax.experimental.pallas import tpu as pltpu
from jax.sharding import PartitionSpec as P

HD = 32
GRID = 14
WIN = 7
SHIFT = 3
LAYERS = 2
TABLE = 169
EPS = 1e-05
MASKED = -100.0
PADDED = -1e30
SLOT = 64
PER_STEP = 2
LANES = 128
EXACT_PRECISION = lax.Precision.HIGHEST
F32 = jnp.float32
BF16 = jnp.bfloat16


def normalize(residual):
    average = jnp.mean(residual, -1, keepdims=True)
    centered = residual - average
    inverse = lax.rsqrt(jnp.mean(centered * centered, -1, keepdims=True) + EPS)
    return (centered * inverse, inverse)


def norm_back(grad_out, normed, inverse, gain_value):
    scaled = grad_out * gain_value
    return inverse * (
        scaled
        - jnp.mean(scaled, -1, keepdims=True)
        - normed * jnp.mean(scaled * normed, -1, keepdims=True)
    )


def gelu_parts(hidden_pre):
    cumulative = 0.5 * (1.0 + lax.erf(hidden_pre * 0.7071067811865476))
    density = jnp.exp(-0.5 * hidden_pre * hidden_pre) * 0.3989422804014327
    return (hidden_pre * cumulative, cumulative + hidden_pre * density)


def dot(a, b, ca=1, cb=0):
    return lax.dot_general(a, b, (((ca,), (cb,)), ((), ())), preferred_element_type=F32)


def stack_heads(block, masks):
    return jnp.concatenate([block * m for m in masks], axis=0)


def merge_heads(stacked, masks):
    total = None
    for h, m in enumerate(masks):
        part = stacked[h * SLOT : (h + 1) * SLOT] * m
        total = part if total is None else total + part
    return total


def head_masks(dtype):
    lane = lax.broadcasted_iota(jnp.int32, (SLOT, LANES), 1)
    return [
        jnp.where((lane >= h * HD) & (lane < (h + 1) * HD), 1.0, 0.0).astype(dtype)
        for h in range(LANES // HD)
    ]


def probabilities(queries_stacked, keys, bias):
    scores = dot(queries_stacked, keys, 1, 1) + bias
    exponent = jnp.exp(scores - jnp.max(scores, -1, keepdims=True))
    return exponent * (1.0 / jnp.sum(exponent, -1, keepdims=True))


def attention_kernel(qkv_ref, bias_ref, mask_ref, out_ref):
    width = out_ref.shape[1]
    low, full = head_masks(BF16), head_masks(F32)
    for g, w in itertools.product(range(width // LANES), range(mask_ref.shape[0])):
        rows = slice(w * SLOT, (w + 1) * SLOT)
        mask = jnp.concatenate([mask_ref[w]] * len(low), axis=0)
        q = qkv_ref[rows, g * LANES : (g + 1) * LANES]
        k = qkv_ref[rows, width + g * LANES : width + (g + 1) * LANES]
        v = qkv_ref[rows, 2 * width + g * LANES : 2 * width + (g + 1) * LANES]
        attention = probabilities(stack_heads(q, low), k, bias_ref[g] + mask)
        mixed = dot(attention.astype(BF16), v)
        out_ref[rows, g * LANES : (g + 1) * LANES] = merge_heads(mixed, full).astype(BF16)


def attention_back_kernel(scale, qkv_ref, dmix_ref, bias_ref, mask_ref, dqkv_ref, dscore_ref, dbias_ref):
    width = dmix_ref.shape[1]
    low, full = head_masks(BF16), head_masks(F32)

    @pl.when(pl.program_id(0) == 0)
    def _():
        dscore_ref[...] = jnp.zeros_like(dscore_ref)
        dbias_ref[...] = jnp.zeros_like(dbias_ref)

    def put(part, g, at_rows, value):
        at = slice(part * width + g * LANES, part * width + (g + 1) * LANES)
        dqkv_ref[at_rows, at] = value.astype(BF16)
        if part != 1:
            rows = value[0:8]
            for r in range(1, SLOT // 8):
                rows = rows + value[r * 8 : (r + 1) * 8]
            dbias_ref[:, at] += rows

    for g, w in itertools.product(range(width // LANES), range(mask_ref.shape[0])):
        rows = slice(w * SLOT, (w + 1) * SLOT)
        mask = jnp.concatenate([mask_ref[w]] * len(low), axis=0)
        q = qkv_ref[rows, g * LANES : (g + 1) * LANES]
        k = qkv_ref[rows, width + g * LANES : width + (g + 1) * LANES]
        v = qkv_ref[rows, 2 * width + g * LANES : 2 * width + (g + 1) * LANES]
        dm = dmix_ref[rows, g * LANES : (g + 1) * LANES]
        q_stacked = stack_heads(q, low)
        dm_stacked = stack_heads(dm, low)
        attention = probabilities(q_stacked, k, bias_ref[g] + mask)
        dattention = dot(dm_stacked, v, 1, 1)
        inner = jnp.sum(attention * dattention, -1, keepdims=True)
        dscores = attention * (dattention - inner)
        dscore_ref[g] += dscores
        dl = dscores.astype(BF16)
        put(0, g, rows, merge_heads(dot(dl, k), full) * scale)
        put(1, g, rows, dot(dl, q_stacked, 0, 0))
        put(2, g, rows, dot(attention.astype(BF16), dm_stacked, 0, 0))


def attention_forward(qkv, bias, mask):
    rows, width = qkv.shape[0], qkv.shape[1] // 3
    windows = mask.shape[0]
    return pl.pallas_call(
        attention_kernel,
        grid=(rows // (PER_STEP * SLOT),),
        out_shape=jax.ShapeDtypeStruct((rows, width), BF16),
        in_specs=[
            pl.BlockSpec((PER_STEP * SLOT, 3 * width), lambda i: (i, 0)),
            pl.BlockSpec(bias.shape, lambda i: (0, 0, 0)),
            pl.BlockSpec((PER_STEP, SLOT, SLOT), lambda i: (lax.rem(i, windows // PER_STEP), 0, 0)),
        ],
        out_specs=pl.BlockSpec((PER_STEP * SLOT, width), lambda i: (i, 0)),
        cost_estimate=pl.CostEstimate(
            flops=rows * width * SLOT * 16, bytes_accessed=rows * width * 8, transcendentals=rows * width * 2
        ),
        name="attention_forward",
    )(qkv, bias, mask)


def attention_backward(qkv, dmix, bias, mask, scale):
    rows, width = dmix.shape
    windows = mask.shape[0]
    return pl.pallas_call(
        functools.partial(attention_back_kernel, scale),
        grid=(rows // (PER_STEP * SLOT),),
        out_shape=(
            jax.ShapeDtypeStruct((rows, 3 * width), BF16),
            jax.ShapeDtypeStruct(bias.shape, F32),
            jax.ShapeDtypeStruct((8, 3 * width), F32),
        ),
        in_specs=[
            pl.BlockSpec((PER_STEP * SLOT, 3 * width), lambda i: (i, 0)),
            pl.BlockSpec((PER_STEP * SLOT, width), lambda i: (i, 0)),
            pl.BlockSpec(bias.shape, lambda i: (0, 0, 0)),
            pl.BlockSpec((PER_STEP, SLOT, SLOT), lambda i: (lax.rem(i, windows // PER_STEP), 0, 0)),
        ],
        out_specs=(
            pl.BlockSpec((PER_STEP * SLOT, 3 * width), lambda i: (i, 0)),
            pl.BlockSpec(bias.shape, lambda i: (0, 0, 0)),
            pl.BlockSpec((8, 3 * width), lambda i: (0, 0)),
        ),
        cost_estimate=pl.CostEstimate(
            flops=rows * width * SLOT * 40, bytes_accessed=rows * width * 16, transcendentals=rows * width * 2
        ),
        name="attention_backward",
    )(qkv, dmix, bias, mask)


def placement(tokens, shift):
    per_side = GRID // WIN
    slots = tokens // (WIN * WIN) * SLOT
    row = lax.broadcasted_iota(jnp.int32, (slots, tokens), 0)
    column = lax.broadcasted_iota(jnp.int32, (slots, tokens), 1)
    window, p = row // SLOT, row % SLOT
    image, w = window // (per_side * per_side), window % (per_side * per_side)
    gi = (w // per_side * WIN + p // WIN + shift) % GRID
    gj = (w % per_side * WIN + p % WIN + shift) % GRID
    source = (
        image * (GRID * GRID)
        + (gi // WIN * per_side + gj // WIN) * (WIN * WIN)
        + gi % WIN * WIN
        + gj % WIN
    )
    return ((column == source) & (p < WIN * WIN)).astype(BF16)


def pack_weights(w_qkv, w_proj, w_fc1, w_fc2):
    rows = w_qkv.shape[1]
    return jnp.concatenate(
        [w_qkv.transpose(1, 0, 2).reshape(rows, -1), w_proj.T, w_fc1, w_fc2.T], axis=1
    )


def per_device(
    inputs,
    cotangent,
    region_ids,
    rel_index,
    norm1_gain,
    norm1_bias,
    w_qkv,
    qv_bias,
    bias_table,
    w_proj,
    proj_bias,
    norm2_gain,
    norm2_bias,
    w_fc1,
    fc1_bias,
    w_fc2,
    fc2_bias,
):
    n_dp, n_t = lax.axis_size("dp"), lax.axis_size("tensor")
    t_index = lax.axis_index("tensor")
    tokens, width = inputs.shape
    ff_local = fc1_bias.shape[1]
    heads_local = bias_table.shape[1]
    heads = heads_local * n_t
    local = heads_local * HD
    shard = width // n_dp
    cuts = (3 * local, 4 * local, 4 * local + ff_local, 4 * local + 2 * ff_local)
    per_side = GRID // WIN
    windows = per_side * per_side
    win_tokens = WIN * WIN
    score_scale = HD ** (-0.5)
    groups = width // LANES

    def pack_grads(g_qkv, g_proj, g_fc1, g_fc2):
        sides = []
        for t in range(n_t):
            pieces = []
            for g, n in ((g_qkv, 3), (g_proj, 1), (g_fc1, 1), (g_fc2, 1)):
                step = g.shape[1] // (n * n_t)
                pieces += [g[:, (m * n_t + t) * step : (m * n_t + t + 1) * step].astype(BF16) for m in range(n)]
            sides.append(jnp.concatenate(pieces, axis=1).reshape(n_dp, shard, -1))
        return jnp.stack(sides, axis=1)

    small = jnp.concatenate([qv_bias.reshape(-1), fc1_bias.reshape(-1), bias_table.reshape(-1)])
    extra = -(-small.shape[0] // (shard * LANES)) * LANES
    small_packed = jnp.pad(small, (0, shard * extra - small.shape[0])).reshape(shard, extra)

    def gather_layer(l):
        packed = pack_weights(w_qkv[l], w_proj[l], w_fc1[l], w_fc2[l])
        if l == 0:
            packed = jnp.concatenate([packed, small_packed], axis=1)
        whole = gather_shards(packed)
        return whole, whole[0, :, :, cuts[3] :].reshape(n_t, -1)

    def unpack_weights(whole):
        blocks = [whole[:, t].reshape(width, -1) for t in range(n_t)]
        parts = []
        lo = 0
        for n, hi in zip((3, 1, 1, 1), cuts):
            step = (hi - lo) // n
            parts.append(
                jnp.concatenate([b[:, lo + m * step : lo + (m + 1) * step] for m in range(n) for b in blocks], axis=1)
            )
            lo = hi
        return parts

    gathered = [gather_layer(l) for l in range(LAYERS)]
    wholes = [whole for whole, _ in gathered]
    weights = [None] * LAYERS
    small = gathered[0][1][:, : small.shape[0]]
    n_qv, n_fc = qv_bias.size, fc1_bias.size
    qv_full = small[:, :n_qv].reshape(n_t, LAYERS, 2, local).transpose(1, 2, 0, 3).reshape(LAYERS, 2, width)
    fc1_full = small[:, n_qv : n_qv + n_fc].reshape(n_t, LAYERS, ff_local).transpose(1, 0, 2).reshape(LAYERS, -1)
    table_full = (
        small[:, n_qv + n_fc :].reshape(n_t, LAYERS, heads_local, TABLE).transpose(1, 0, 2, 3).reshape(LAYERS, heads, TABLE)
    ).astype(F32)
    fc1_full = fc1_full.astype(F32)
    qv_full = qv_full.astype(F32)

    pad = SLOT - win_tokens
    index_padded = jnp.pad(rel_index, ((0, pad), (0, pad)), constant_values=-1).reshape(-1)
    one_hot = (index_padded[None, :] == jnp.arange(TABLE, dtype=jnp.int32)[:, None]).astype(F32)
    regions = region_ids.reshape(windows, win_tokens)
    shift_mask = jnp.where(regions[:, :, None] == regions[:, None, :], 0.0, MASKED).astype(F32)

    def padded_mask(mask):
        return jnp.pad(
            jnp.pad(mask, ((0, 0), (0, pad), (0, 0))), ((0, 0), (0, 0), (0, pad)), constant_values=PADDED
        )

    masks = [padded_mask(jnp.zeros_like(shift_mask)), padded_mask(shift_mask)]
    biases = [
        jnp.dot(table_full[l], one_hot, precision=EXACT_PRECISION).reshape(groups, LANES // HD * SLOT, SLOT)
        for l in range(LAYERS)
    ]
    places = [placement(tokens, SHIFT * (l % 2)) for l in range(LAYERS)]
    scale_row = jnp.concatenate([jnp.full((width,), score_scale, F32), jnp.ones((2 * width,), F32)])

    residual = inputs.astype(F32)
    store = []
    for l in range(LAYERS):
        whole, residual = lax.optimization_barrier((wholes[l], residual)) if l else (wholes[l], residual)
        weights[l] = unpack_weights(whole)
        qkv_w, proj_w, fc1_w, fc2_w = weights[l]
        place = places[l]
        normed1, inverse1 = normalize(residual)
        attn_in = (normed1 * norm1_gain[l].astype(F32) + norm1_bias[l].astype(F32)).astype(BF16)
        attn_pad = dot(place, attn_in).astype(BF16)
        qkv_bias = jnp.concatenate([qv_full[l, 0], jnp.zeros((width,), F32), qv_full[l, 1]])
        qkv = ((dot(attn_pad, qkv_w) + qkv_bias) * scale_row).astype(BF16)
        mixture = dot(place, attention_forward(qkv, biases[l], masks[l % 2]), 0, 0).astype(BF16)
        residual_mid = residual + dot(mixture, proj_w, 1, 1) + proj_bias[l].astype(F32)
        normed2, inverse2 = normalize(residual_mid)
        ffn_in = (normed2 * norm2_gain[l].astype(F32) + norm2_bias[l].astype(F32)).astype(BF16)
        activated, slope = gelu_parts(dot(ffn_in, fc1_w) + fc1_full[l])
        hidden = activated.astype(BF16)
        slope = slope.astype(BF16)
        store.append((normed1, inverse1, attn_in, qkv, mixture, normed2, inverse2, ffn_in, slope, hidden))
        residual = residual_mid + dot(hidden, fc2_w, 1, 1) + fc2_bias[l].astype(F32)

    g = cotangent.astype(F32)
    weight_grads = [None] * LAYERS
    small_grads = [None] * LAYERS
    for l in reversed(range(LAYERS)):
        qkv_w, proj_w, fc1_w, fc2_w = weights[l]
        place = places[l]
        normed1, inverse1, attn_in, qkv, mixture, normed2, inverse2, ffn_in, slope, hidden = store[l]
        g_fc2_bias = jnp.sum(g, 0)
        gl = g.astype(BF16)
        dpre = dot(gl, fc2_w) * slope.astype(F32)
        dpl = dpre.astype(BF16)
        g_fc1_bias = jnp.sum(dpre, 0)
        g_fc2 = dot(gl, hidden, 0, 0)
        g_fc1 = dot(ffn_in, dpl, 0, 0)
        dffn = dot(dpl, fc1_w, 1, 1)
        g_n2_gain = jnp.sum(dffn * normed2, 0)
        g_n2_bias = jnp.sum(dffn, 0)
        g_mid = g + norm_back(dffn, normed2, inverse2, norm2_gain[l].astype(F32))
        g_proj_bias = jnp.sum(g_mid, 0)
        gm = g_mid.astype(BF16)
        g_proj = dot(gm, mixture, 0, 0)
        dmix = dot(gm, proj_w).astype(BF16)
        dmix_pad = dot(place, dmix).astype(BF16)
        dqkv_pad, dscores, dbias = attention_backward(qkv, dmix_pad, biases[l], masks[l % 2], score_scale)
        g_table = lax.dot_general(
            dscores.reshape(heads, SLOT * SLOT), one_hot, (((1,), (1,)), ((), ())), precision=EXACT_PRECISION
        )
        dqkv = dot(place, dqkv_pad, 0, 0).astype(BF16)
        g_qkv = dot(attn_in, dqkv, 0, 0)
        dattn = dot(dqkv, qkv_w, 1, 1)
        g_n1_gain = jnp.sum(dattn * normed1, 0)
        g_n1_bias = jnp.sum(dattn, 0)
        g = g_mid + norm_back(dattn, normed1, inverse1, norm1_gain[l].astype(F32))
        dbias_rows = jnp.sum(dbias, 0)
        weight_grads[l] = reduce_shards(pack_grads(g_qkv, g_proj, g_fc1, g_fc2)).astype(F32)
        small_grads[l] = [
            g_n1_gain, g_n1_bias, g_proj_bias, g_n2_gain, g_n2_bias, g_fc2_bias,
            dbias_rows[:width], dbias_rows[2 * width :], g_fc1_bias, g_table.reshape(-1),
        ]

    flat = jnp.concatenate([v for l in range(LAYERS) for v in small_grads[l]])
    total = sum_everywhere(flat).reshape(LAYERS, -1)
    vectors = total[:, : 6 * width].reshape(LAYERS, 6, width)
    at = 6 * width
    qv_total = total[:, at : at + 2 * width].reshape(LAYERS, 2, width)
    qv_total = lax.dynamic_slice_in_dim(qv_total, t_index * local, local, 2)
    at += 2 * width
    fc1_total = lax.dynamic_slice_in_dim(total[:, at : at + ff_local * n_t], t_index * ff_local, ff_local, 1)
    at += ff_local * n_t
    table_total = lax.dynamic_slice_in_dim(
        total[:, at:].reshape(LAYERS, heads, TABLE), t_index * heads_local, heads_local, 1
    )
    grads = jnp.stack(weight_grads)
    qkv_total = grads[..., : cuts[0]].reshape(LAYERS, shard, 3, local).transpose(0, 2, 1, 3)
    proj_w_total = grads[..., cuts[0] : cuts[1]].transpose(0, 2, 1)
    fc1_w_total = grads[..., cuts[1] : cuts[2]]
    fc2_w_total = grads[..., cuts[2] :].transpose(0, 2, 1)
    return (
        residual,
        g,
        vectors[:, 0],
        vectors[:, 1],
        qkv_total,
        qv_total,
        table_total,
        proj_w_total,
        vectors[:, 2],
        vectors[:, 3],
        vectors[:, 4],
        fc1_w_total,
        fc1_total,
        fc2_w_total,
        vectors[:, 5],
    )


def gather_shards(packed):
    n_dp, n_t = lax.axis_size("dp"), lax.axis_size("tensor")
    rows = lax.all_gather(packed, ("dp", "tensor"), axis=0, tiled=False)
    return rows.reshape((n_dp, n_t) + packed.shape)


def reduce_shards(packed):
    rows = packed.reshape((-1,) + packed.shape[2:])
    return lax.psum_scatter(rows, ("dp", "tensor"), scatter_dimension=0, tiled=False)


def partners():
    found = []
    for axis in ("tensor", "dp"):
        size, bit = lax.axis_size(axis), 1
        assert size & (size - 1) == 0
        me = lax.axis_index(axis)
        while bit < size:
            found.append((axis, me + bit - 2 * bit * ((me // bit) % 2)))
            bit *= 2
    return found


def exchange_kernel(x_ref, out_ref, held, arrived, send_sem, recv_sem):
    steps = partners()
    barrier = pltpu.get_barrier_semaphore()
    for axis, place in steps:
        pl.semaphore_signal(barrier, inc=1, device_id={axis: place}, device_id_type=pl.DeviceIdType.MESH)
    pl.semaphore_wait(barrier, len(steps))
    for s, (axis, place) in enumerate(steps):
        source = x_ref if s == 0 else held.at[s - 1]
        copy = pltpu.make_async_remote_copy(
            src_ref=source,
            dst_ref=arrived.at[s],
            send_sem=send_sem.at[s],
            recv_sem=recv_sem.at[s],
            device_id={axis: place},
            device_id_type=pl.DeviceIdType.MESH,
        )
        copy.start()
        copy.wait()
        total = source[...] + arrived[s]
        if s < len(steps) - 1:
            held[s] = total
        else:
            out_ref[...] = total


def sum_everywhere(flat):
    size = flat.shape[0]
    rows = -(-size // (8 * LANES)) * 8
    x = jnp.pad(flat, (0, rows * LANES - size)).reshape(rows, LANES)
    n = len(partners())
    total = pl.pallas_call(
        exchange_kernel,
        out_shape=jax.ShapeDtypeStruct(x.shape, F32),
        in_specs=[pl.BlockSpec(memory_space=pltpu.VMEM)],
        out_specs=pl.BlockSpec(memory_space=pltpu.VMEM),
        scratch_shapes=[
            pltpu.VMEM((n,) + x.shape, F32),
            pltpu.VMEM((n,) + x.shape, F32),
            pltpu.SemaphoreType.DMA((n,)),
            pltpu.SemaphoreType.DMA((n,)),
        ],
        compiler_params=pltpu.CompilerParams(collective_id=0, has_side_effects=True),
        name="sum_everywhere",
    )(x)
    return total.reshape(-1)[:size]


SMALL_ROWS = 24
TABLE_LANES = 256
PACK = LANES // HD
PARAMS = ("n1g", "n1b", "pb", "n2g", "n2b", "f2b")


def flip(index, bit):
    return index + bit - 2 * bit * ((index // bit) % 2)


def mix(index, j):
    bit = 1
    while bit <= j:
        if j & bit:
            index = flip(index, bit)
        bit *= 2
    return index


def shift_segments(shift):
    per_side = GRID // WIN
    moves = []
    for w in range(per_side * per_side):
        for p in range(WIN * WIN):
            gi = (w // per_side * WIN + p // WIN + shift) % GRID
            gj = (w % per_side * WIN + p % WIN + shift) % GRID
            source = (gi // WIN * per_side + gj // WIN) * SLOT + gi % WIN * WIN + gj % WIN
            moves.append((w * SLOT + p, source))
    runs = []
    for target, source in moves:
        if runs and runs[-1][0] + runs[-1][2] == target and runs[-1][1] + runs[-1][2] == source:
            runs[-1][2] += 1
        else:
            runs.append([target, source, 1])
    return runs


class Plan:
    def __init__(self, n_dp, tokens, width, ff_local, heads_local):
        self.Y = self.X = 2
        self.Z = n_dp // 4
        self.T = 2
        self.width = width
        self.shard = width // n_dp
        self.local = heads_local * HD
        self.heads_local = heads_local
        self.ffl = ff_local
        self.cols = 4 * self.local + 2 * ff_local
        self.windows = (GRID // WIN) ** 2
        self.images = tokens // (GRID * GRID)
        self.block = self.windows * SLOT
        self.rows = self.images * self.block
        self.groups = self.T * self.local // LANES
        a, b, c = 3 * self.local, 4 * self.local, 4 * self.local + ff_local
        self.at = {"qkv": (0, a), "proj": (a, b), "fc1": (b, c), "fc2": (c, self.cols)}
        self.gather_chunks = [(0, a), (a, c), (c, self.cols)]
        self.scatter_chunks = {"qkv": (0, a), "proj": (a, b), "fc1": (b, c), "fc2": (c, self.cols)}


def halves(cut):
    lo, hi = cut
    step = (hi - lo) // 2 // LANES * LANES
    return ((lo, step), (lo + step, hi - lo - step))


def step_kernel(plan, *refs):
    (x_ref, cot_ref, shard_ref, vec_ref, tab_ref, par_ref, mask_ref, hot_ref,
     out_ref, gin_ref, grad_ref, tot_ref, spill_big, spill_small, spill_inv, spill_qkv,
     W, G1, vecs, tabs, big, low, inv, qkv, gl, mid, bias, dscore, dbias, small, part,
     R0, R1, R2, R3, SR,
     ag_send, ag_recv, rs_send, rs_recv, sm_send, sm_recv, sp_sem) = refs
    Z, T, width, local, ffl = plan.Z, plan.T, plan.width, plan.local, plan.ffl
    block, images, rows = plan.block, plan.images, plan.rows
    L = LAYERS
    dp, t = lax.axis_index("dp"), lax.axis_index("tensor")
    z, y, x = dp // 4, (dp // 2) % 2, dp % 2
    other = 1 - t
    MESH = pl.DeviceIdType.MESH
    to_z = [{"dp": dp + 4 * (mix(z, j) - z)} for j in range(1, Z)]
    to_y, to_x, to_t = {"dp": flip(dp, 2)}, {"dp": flip(dp, 1)}, {"tensor": other}
    pending = []

    def remote(src, dst, send, recv, device):
        return pltpu.make_async_remote_copy(
            src_ref=src, dst_ref=dst, send_sem=send, recv_sem=recv, device_id=device, device_id_type=MESH
        )

    barrier = pltpu.get_barrier_semaphore()
    for device in to_z + [to_y, to_x, to_t]:
        pl.semaphore_signal(barrier, inc=1, device_id=device, device_id_type=MESH)

    xb = [(l, c) for l in range(L) for c in range(len(plan.gather_chunks))]

    def ag_copies(l, c):
        found = []
        for h, (lo, n) in enumerate(halves(plan.gather_chunks[c])):
            k = (l * len(plan.gather_chunks) + c) * 2 + h
            cs = pl.ds(lo, n)
            own = W.at[l, t, z, y, x, :, cs]
            plane = W.at[l, t, :, y, x, :, cs]
            if h == 0:
                wide, new2, new3 = W.at[l, t, :, :, x, :, cs], W.at[l, t, :, 1 - y, x, :, cs], W.at[l, t, :, :, 1 - x, :, cs]
                first, second = to_y, to_x
            else:
                wide, new2, new3 = W.at[l, t, :, y, :, :, cs], W.at[l, t, :, y, 1 - x, :, cs], W.at[l, t, :, 1 - y, :, :, cs]
                first, second = to_x, to_y
            s = lambda i, k=k: (ag_send.at[k, i], ag_recv.at[k, i])
            found.append(dict(
                p1=[remote(shard_ref.at[l, :, cs], own, *s(j), to_z[j]) for j in range(Z - 1)],
                p2=[remote(plane, plane, *s(Z - 1), first)],
                p3=[remote(wide, wide, *s(Z), second)],
                f1=[remote(plane, plane, *s(Z + 1), to_t)],
                f2=[remote(new2, new2, *s(Z + 2), to_t)],
                f3=[remote(new3, new3, *s(Z + 3), to_t)],
            ))
        return found

    def begin(copies):
        for copy in copies:
            copy.start()

    def arrive(copies):
        for copy in copies:
            copy.wait_recv()

    gathers = {key: ag_copies(*key) for key in xb}

    def ag(key, stage):
        for half in gathers[key]:
            if stage == 1:
                begin(half["p1"])
            elif stage == 2:
                arrive(half["p1"])
                begin(half["p2"] + half["f1"])
            elif stage == 3:
                arrive(half["p2"])
                begin(half["p3"] + half["f2"])
            elif stage == 4:
                arrive(half["p3"])
                begin(half["f3"])
            else:
                arrive(half["f1"] + half["f2"] + half["f3"])

    names = ("fc2", "fc1", "proj", "qkv")

    def grads_of(l):
        return G1 if l == L - 1 else W.at[L - 1]

    def rs_copies(l, name):
        found = []
        G = grads_of(l)
        for h, (lo, n) in enumerate(halves(plan.scatter_chunks[name])):
            k = (l * len(names) + names.index(name)) * 2 + h
            cs = pl.ds(lo, n)
            s = lambda i, k=k: (rs_send.at[k, i], rs_recv.at[k, i])
            if h == 0:
                away1, away2, first, second = G.at[t, :, :, 1 - x, :, cs], G.at[t, :, 1 - y, x, :, cs], to_x, to_y
            else:
                away1, away2, first, second = G.at[t, :, 1 - y, :, :, cs], G.at[t, :, y, 1 - x, :, cs], to_y, to_x
            found.append((cs, h, [
                [remote(G.at[other, :, :, :, :, cs], R0.at[l, :, :, :, :, cs], *s(0), to_t)],
                [remote(away1, R1.at[l, :, :, :, cs], *s(1), first)],
                [remote(away2, R2.at[l, :, :, cs], *s(2), second)],
                [remote(G.at[t, mix(z, j), y, x, :, cs], R3.at[l, j - 1, :, cs], *s(2 + j), to_z[j - 1]) for j in range(1, Z)],
            ]))
        return found

    scatters = {(l, name): rs_copies(l, name) for l in range(L) for name in names}

    def plus(a, b):
        return (a.astype(F32) + b.astype(F32)).astype(BF16)

    def rs(key, stage):
        l = key[0]
        G = grads_of(l)
        for cs, h, copies in scatters[key]:
            if stage > 0:
                arrive(copies[stage - 1])
            if stage == 1:
                @pl.loop(0, Z)
                def _(i):
                    G[t, i, :, :, :, cs] = plus(G[t, i, :, :, :, cs], R0[l, i, :, :, :, cs])
            elif stage == 2:
                @pl.loop(0, Z)
                def _(i):
                    for m in range(2):
                        where = (t, i, m, x) if h == 0 else (t, i, y, m)
                        G[(*where, slice(None), cs)] = plus(G[(*where, slice(None), cs)], R1[l, i, m, :, cs])
            elif stage == 3:
                @pl.loop(0, Z)
                def _(i):
                    G[t, i, y, x, :, cs] = plus(G[t, i, y, x, :, cs], R2[l, i, :, cs])
            elif stage == 4:
                total = G[t, z, y, x, :, cs].astype(F32)
                for j in range(1, Z):
                    total = total + R3[l, j - 1, :, cs].astype(F32)
                grad_ref[l, :, cs] = total
            if stage < 4:
                begin(copies[stage])

    def sm_copies():
        s = lambda i: (sm_send.at[i], sm_recv.at[i])
        found = [[remote(part.at[0], SR.at[0], *s(0), to_t)]]
        found.append([remote(part.at[1], SR.at[1], *s(1), to_x)])
        found.append([remote(part.at[2], SR.at[2], *s(2), to_y)])
        found.append([remote(part.at[3], SR.at[2 + j], *s(2 + j), to_z[j - 1]) for j in range(1, Z)])
        return found

    sums = sm_copies()

    def sm(stage):
        if stage > 0:
            arrive(sums[stage - 1])
        if stage == 0:
            part[0] = small[...]
        elif stage < 4:
            part[stage] = part[stage - 1] + SR[stage - 1]
        else:
            level = [part[3]] + [SR[2 + j] for j in range(1, Z)]
            while len(level) > 1:
                level = [level[i] + level[i + 1] for i in range(0, len(level), 2)]
            tot_ref[...] = level[0]
        if stage < 4:
            begin(sums[stage])

    queue = []

    def tick(n=1):
        while n > 0 and queue:
            item = queue.pop(0)
            if item is not None:
                item()
                n -= 1

    def drain_to(mark):
        while any(getattr(item, "mark", None) == mark for item in queue):
            item = queue.pop(0)
            if item is not None:
                item()

    def push(fn, *args, mark=None):
        item = functools.partial(fn, *args)
        item.mark = mark
        queue.append(item)

    def gap(n=1):
        queue.extend([None] * n)

    def spread(i, count, each=1):
        for k in range(count):
            taken = [item for item in (queue.pop(0) for _ in range(min(each, len(queue)))) if item is not None]
            if taken:
                @pl.when(i == k)
                def _(taken=taken):
                    for item in taken:
                        item()

    def weight(l, tt, name, lo=None, n=None):
        a, b = plan.at[name]
        value = W[l, tt, :, :, :, :, a:b]
        return value.reshape(width, b - a)

    def put_grad(l, tt, name, first, value):
        a, b = plan.at[name]
        zs = value.shape[0] // (4 * plan.shard)
        grads_of(l)[tt, pl.ds(first, zs), :, :, :, a:b] = value.astype(BF16).reshape(zs, 2, 2, plan.shard, b - a)

    def row_slice(i):
        return pl.ds(pl.multiple_of(i * block, block), block)

    def param(l, name):
        return par_ref[l, PARAMS.index(name)][None, :]

    def add_small(l, row, value, lanes=slice(0, width)):
        small[l, row : row + 1, lanes] += jnp.sum(value, 0, keepdims=True)

    def permute(target, source, shift):
        runs = shift_segments(shift)

        @pl.loop(0, images)
        def _(i):
            base = pl.multiple_of(i * block, block)
            target[pl.ds(base, block), :] = jnp.zeros((block, width), F32)
            src, dst = source.at[pl.ds(base, block)], target.at[pl.ds(base, block)]
            for to, frm, n in runs:
                dst[to : to + n, :] = src[frm : frm + n, :]

    X1, AIN, MIX, X2, FIN = range(5)
    HID, SLOPE = 0, 1
    per = local // LANES

    def group_at(g, part_index):
        return (g // per) * 3 * local + part_index * local + (g % per) * LANES

    scale = HD ** (-0.5)
    low_masks, full_masks = head_masks(BF16), head_masks(F32)

    def win_rows(w):
        return pl.ds(pl.multiple_of(w * SLOT, SLOT), SLOT)

    def load_group(w, g):
        r = win_rows(w)
        return [qkv[r, group_at(g, n) : group_at(g, n) + LANES] for n in range(3)]

    def bias_of(l, w, g):
        if l % 2 == 0:
            return bias[l * plan.groups + g]
        return bias[(lax.rem(w, plan.windows) + 1) * plan.groups + g]

    def column_softmax(scores):
        exponent = jnp.exp(scores - jnp.max(scores, 0, keepdims=True))
        return exponent * (1.0 / jnp.sum(exponent, 0, keepdims=True))

    def pick_heads(stacked):
        lane = lax.broadcasted_iota(jnp.int32, (SLOT, LANES), 1)
        out = stacked[(PACK - 1) * SLOT :]
        for h in range(PACK - 2, -1, -1):
            out = jnp.where(lane < (h + 1) * HD, stacked[h * SLOT : (h + 1) * SLOT], out)
        return out

    def forward(l, r):
        @pl.loop(0, images)
        def _(i):
            rs_ = row_slice(i)
            normed, inverse = normalize(r[rs_, :])
            low[X1, rs_, :] = normed.astype(BF16)
            inv[0, rs_, :] = inverse
            low[AIN, rs_, :] = (normed * param(l, "n1g") + param(l, "n1b")).astype(BF16)

        if l == 0:
            prepare()
            drain_to((0, 0))
        else:
            drain_to((l, 0))

        @pl.loop(0, images)
        def _(i):
            rs_ = row_slice(i)
            a = low[AIN, rs_, :]
            for tt in range(T):
                value = dot(a, weight(l, tt, "qkv"))
                at = tt * 3 * local
                qb = vecs[tt, l, 1:2, 0:local]
                vb = vecs[tt, l, 2:3, 0:local]
                qkv[rs_, at : at + local] = ((value[:, :local] + qb) * scale).astype(BF16)
                qkv[rs_, at + local : at + 2 * local] = value[:, local : 2 * local].astype(BF16)
                qkv[rs_, at + 2 * local : at + 3 * local] = (value[:, 2 * local :] + vb).astype(BF16)
            spread(i, images)

        @pl.loop(0, images * plan.windows)
        def _(w):
            for g in range(plan.groups):
                q, k, v = load_group(w, g)
                attention = column_softmax(dot(k, stack_heads(q, low_masks), 1, 1) + bias_of(l, w, g))
                mixed = dot(attention.astype(BF16), v, 0, 0)
                low[MIX, win_rows(w), g * LANES : (g + 1) * LANES] = pick_heads(mixed).astype(BF16)
            spread(w, images * plan.windows)

        drain_to((l, 1))

        @pl.loop(0, images)
        def _(i):
            rs_ = row_slice(i)
            total = r[rs_, :] + param(l, "pb")
            for tt in range(T):
                total = total + dot(low[MIX, rs_, tt * local : (tt + 1) * local], weight(l, tt, "proj"), 1, 1)
            r[rs_, :] = total
            normed, inverse = normalize(total)
            low[X2, rs_, :] = normed.astype(BF16)
            inv[1, rs_, :] = inverse
            low[FIN, rs_, :] = (normed * param(l, "n2g") + param(l, "n2b")).astype(BF16)

        for tt in range(T):
            @pl.loop(0, images)
            def _(i, tt=tt):
                rs_ = row_slice(i)
                pre = dot(low[FIN, rs_, :], weight(l, tt, "fc1")) + vecs[tt, l, 0:1, :]
                activated, slope = gelu_parts(pre)
                big[HID, rs_, tt * ffl : (tt + 1) * ffl] = activated.astype(BF16)
                big[SLOPE, rs_, tt * ffl : (tt + 1) * ffl] = slope.astype(BF16)
                spread(i, images)

        drain_to((l, 2))

        @pl.loop(0, images)
        def _(i):
            rs_ = row_slice(i)
            total = r[rs_, :] + param(l, "f2b")
            for tt in range(T):
                total = total + dot(big[HID, rs_, tt * ffl : (tt + 1) * ffl], weight(l, tt, "fc2"), 1, 1)
            r[rs_, :] = total
            spread(i, images)

    def prepare():
        bias[...] = jnp.zeros_like(bias)
        for tt in range(T):
            @pl.when(t == tt)
            def _(tt=tt):
                vecs[tt] = vec_ref[...]
                tabs[tt] = tab_ref[...]
        arrive(small_in)

        heads = T * plan.heads_local
        table = jnp.concatenate([tabs[tt, l] for l in range(L) for tt in range(T)], axis=0).astype(BF16)
        shape = (L * heads, PACK * SLOT)
        own = lax.broadcasted_iota(jnp.int32, shape, 0) % PACK == lax.broadcasted_iota(jnp.int32, shape, 1) // SLOT
        shape = (L * plan.groups, L * heads)
        gather = (lax.broadcasted_iota(jnp.int32, shape, 1) // PACK == lax.broadcasted_iota(jnp.int32, shape, 0)).astype(BF16)

        @pl.loop(0, WIN)
        def _(a):
            for b in range(WIN):
                j = a * WIN + b
                line = dot(table, jnp.concatenate([hot_ref[j]] * PACK, axis=0), 1, 1)
                line = dot(gather, jnp.where(own, line, 0.0).astype(BF16))
                bias[0 : L * plan.groups, pl.ds(j, 1), :] = line[:, None, :]
            spread(a, WIN)

        for w in reversed(range(plan.windows)):
            for g in range(plan.groups):
                bias[(w + 1) * plan.groups + g] = bias[plan.groups + g] + mask_ref[w + 1]
        for g in range(plan.groups):
            bias[g] = bias[g] + mask_ref[0]

    def backward(l, g):
        @pl.loop(0, images)
        def _(i):
            rs_ = row_slice(i)
            value = g[rs_, :]
            add_small(l, 5, value)
            gl[rs_, :] = value.astype(BF16)

        half = width // 2
        for tt in range(T):
            fcols = slice(tt * ffl, (tt + 1) * ffl)

            @pl.loop(0, images)
            def _(i, tt=tt, fcols=fcols):
                rs_ = row_slice(i)
                dpre = dot(gl[rs_, :], weight(l, tt, "fc2")) * big[SLOPE, rs_, fcols].astype(F32)
                sums_ = jnp.sum(dpre, 0, keepdims=True)
                for m in range(ffl // width):
                    small[l, 8 + tt * (ffl // width) + m : 9 + tt * (ffl // width) + m, :] += sums_[:, m * width : (m + 1) * width]
                big[SLOPE, rs_, fcols] = dpre.astype(BF16)
                spread(i, images)

            @pl.loop(0, 2)
            def _(m, tt=tt, fcols=fcols):
                lanes = pl.ds(pl.multiple_of(m * half, half), half)
                put_grad(l, tt, "fc2", m * (Z // 2), dot(gl[:, lanes], big[HID, :, fcols], 0, 0))
                spread(m, 2)

        rs((l, "fc2"), 0)
        for tt in range(T):
            fcols = slice(tt * ffl, (tt + 1) * ffl)

            @pl.loop(0, 2)
            def _(m, tt=tt, fcols=fcols):
                lanes = pl.ds(pl.multiple_of(m * half, half), half)
                put_grad(l, tt, "fc1", m * (Z // 2), dot(low[FIN, :, lanes], big[SLOPE, :, fcols], 0, 0))
                spread(m, 2)

        rs((l, "fc1"), 0)
        gap(1)
        push(rs, (l, "fc2"), 1)
        gap(1)
        push(rs, (l, "fc1"), 1)
        push(rs, (l, "fc2"), 2)
        gap(3)
        push(rs, (l, "fc1"), 2)
        push(rs, (l, "fc2"), 3)
        push(rs, (l, "proj"), 1)
        gap(1)
        push(rs, (l, "fc1"), 3)
        push(rs, (l, "proj"), 2)
        push(rs, (l, "fc2"), 4)
        gap(1)
        push(rs, (l, "proj"), 3)
        push(rs, (l, "fc1"), 4)
        push(rs, (l, "proj"), 4)
        gap(2)

        @pl.loop(0, images)
        def _(i):
            rs_ = row_slice(i)
            dffn = dot(big[SLOPE, rs_, 0:ffl], weight(l, 0, "fc1"), 1, 1)
            for tt in range(1, T):
                dffn = dffn + dot(big[SLOPE, rs_, tt * ffl : (tt + 1) * ffl], weight(l, tt, "fc1"), 1, 1)
            normed = low[X2, rs_, :].astype(F32)
            add_small(l, 3, dffn * normed)
            add_small(l, 4, dffn)
            g_mid = g[rs_, :] + norm_back(dffn, normed, inv[1, rs_, :], param(l, "n2g"))
            add_small(l, 2, g_mid)
            g[rs_, :] = g_mid
            gl[rs_, :] = g_mid.astype(BF16)
            spread(i, images)

        if l > 0:
            fetch("big")
        for tt in range(T):
            @pl.loop(0, 2)
            def _(m, tt=tt):
                lanes = pl.ds(pl.multiple_of(m * half, half), half)
                put_grad(l, tt, "proj", m * (Z // 2), dot(gl[:, lanes], low[MIX, :, tt * local : (tt + 1) * local], 0, 0))
        rs((l, "proj"), 0)
        @pl.loop(0, images)
        def _(i):
            rs_ = row_slice(i)
            for tt in range(T):
                low[MIX, rs_, tt * local : (tt + 1) * local] = dot(gl[rs_, :], weight(l, tt, "proj")).astype(BF16)

        dscore[...] = jnp.zeros_like(dscore)
        dbias[...] = jnp.zeros_like(dbias)

        @pl.loop(0, images * plan.windows)
        def _(w):
            r = win_rows(w)
            for gg in range(plan.groups):
                q, k, v = load_group(w, gg)
                dm = low[MIX, r, gg * LANES : (gg + 1) * LANES]
                q_stacked, dm_stacked = stack_heads(q, low_masks), stack_heads(dm, low_masks)
                attention = column_softmax(dot(k, q_stacked, 1, 1) + bias_of(l, w, gg))
                dattention = dot(v, dm_stacked, 1, 1)
                inner = jnp.sum(attention * dattention, 0, keepdims=True)
                dscores = attention * (dattention - inner)
                dscore[gg] += dscores
                dl = dscores.astype(BF16)
                dq = pick_heads(dot(dl, k, 0, 0)) * scale
                dk = dot(dl, q_stacked)
                dv = dot(attention.astype(BF16), dm_stacked)
                for n, value in enumerate((dq, dk, dv)):
                    qkv[r, group_at(gg, n) : group_at(gg, n) + LANES] = value.astype(BF16)
                    if n != 1:
                        dbias[n // 2, :, gg * LANES : (gg + 1) * LANES] += jnp.sum(value.reshape(SLOT // 8, 8, LANES), 0)
            spread(w, images * plan.windows)

        add_small(l, 6, dbias[0])
        add_small(l, 7, dbias[1])
        if l > 0:
            fetch("mix")
        for tt in range(T):
            at = tt * 3 * local

            @pl.loop(0, 2)
            def _(m, tt=tt, at=at):
                lanes = pl.ds(pl.multiple_of(m * half, half), half)
                put_grad(l, tt, "qkv", m * (Z // 2), dot(low[AIN, :, lanes], qkv[:, at : at + 3 * local], 0, 0))
        rs((l, "qkv"), 0)
        gap(4)
        push(rs, (l, "qkv"), 1)
        gap(5)
        push(rs, (l, "qkv"), 2)
        if l > 0:
            gap(4)
        push(rs, (l, "qkv"), 3)
        if l > 0:
            gap(4)
        push(rs, (l, "qkv"), 4)

        spare = 8
        shape = (PACK * spare, PACK * SLOT)
        own = lax.broadcasted_iota(jnp.int32, shape, 0) // spare == lax.broadcasted_iota(jnp.int32, shape, 1) // SLOT

        def table_step(a, acc):
            for b in range(WIN):
                j = a * WIN + b
                line = dscore[:, pl.ds(j, 1), :].reshape(spare, PACK * SLOT)
                line = jnp.where(own, jnp.concatenate([line] * PACK, axis=0), 0.0)
                high = line.astype(BF16)
                rest = line - high.astype(F32)
                middle = rest.astype(BF16)
                least = (rest - middle.astype(F32)).astype(BF16)
                three = jnp.concatenate([high, middle, least], axis=0)
                out = dot(three, jnp.concatenate([hot_ref[j]] * PACK, axis=0))
                n = PACK * spare
                acc = acc + ((out[2 * n :] + out[n : 2 * n]) + out[:n])
            spread(a, WIN)
            return acc

        total = lax.fori_loop(0, WIN, table_step, jnp.zeros((PACK * spare, TABLE_LANES), F32))
        for hh in range(PACK):
            to, lanes = 16 + hh % 2 * plan.groups, slice(hh // 2 * TABLE_LANES, (hh // 2 + 1) * TABLE_LANES)
            small[l, to : to + plan.groups, lanes] = total[hh * spare : hh * spare + plan.groups]

        @pl.loop(0, images)
        def _(i):
            rs_ = row_slice(i)
            dattn = dot(qkv[rs_, 0 : 3 * local], weight(l, 0, "qkv"), 1, 1)
            for tt in range(1, T):
                dattn = dattn + dot(qkv[rs_, tt * 3 * local : (tt + 1) * 3 * local], weight(l, tt, "qkv"), 1, 1)
            normed = low[X1, rs_, :].astype(F32)
            add_small(l, 0, dattn * normed)
            add_small(l, 1, dattn)
            g[rs_, :] = g[rs_, :] + norm_back(dattn, normed, inv[0, rs_, :], param(l, "n1g"))
            spread(i, images)

        if l > 0:
            fetch("rest")

    lows = [(low.at[n], spill_small.at[n]) for n in range(5)]
    moves = {
        "ain": [lows[X1], lows[AIN]], "mix": [lows[MIX], lows[X2], lows[FIN]],
        "inv": [(inv, spill_inv)], "qkv": [(qkv, spill_qkv)], "big": [(big, spill_big)],
    }
    order = [pair for name in ("ain", "mix", "inv", "qkv", "big") for pair in moves[name]]
    fetched = []

    def spill():
        copies = [pltpu.make_async_copy(a, b, sp_sem.at[n]) for n, (a, b) in enumerate(order)]
        begin(copies)
        for copy in copies:
            copy.wait()

    def fetch(name):
        which = {
            "big": [7, 3, 4], "mix": [2], "rest": [0, 1, 5, 6],
        }[name]
        for n in which:
            a, b = order[n]
            copy = pltpu.make_async_copy(b, a, sp_sem.at[n])
            copy.start()
            fetched.append(copy)

    def sent(found):
        for copies in found:
            for half in copies:
                for group in half.values():
                    for copy in group:
                        copy.wait_send()

    small_in = [
        remote(vec_ref, vecs.at[t], sm_send.at[2 + Z], sm_recv.at[2 + Z], to_t),
        remote(tab_ref, tabs.at[t], sm_send.at[3 + Z], sm_recv.at[3 + Z], to_t),
    ]
    pl.semaphore_wait(barrier, Z - 1 + 3)
    ag((0, 0), 1)
    begin(small_in)
    for l in range(L):
        W[l, t, z, y, x] = shard_ref[l]
    small[...] = jnp.zeros_like(small)

    gap(1)
    push(ag, (0, 0), 2)
    push(ag, (0, 1), 1)
    push(ag, (0, 0), 3)
    gap(3)
    push(ag, (0, 0), 4)
    push(ag, (0, 2), 1)
    push(ag, (0, 0), 5, mark=(0, 0))
    push(ag, (0, 1), 2)
    gap(3)
    push(ag, (0, 1), 3)
    push(ag, (0, 2), 2)
    push(ag, (1, 0), 1)
    gap(11)
    push(ag, (0, 1), 4)
    push(ag, (0, 2), 3)
    push(ag, (0, 1), 5, mark=(0, 1))
    push(ag, (1, 1), 1)
    gap(1)
    push(ag, (0, 2), 4)
    push(ag, (1, 0), 2)
    push(ag, (1, 0), 3)
    push(ag, (1, 2), 1)
    gap(1)
    push(ag, (1, 0), 4)
    push(ag, (0, 2), 5, mark=(0, 2))
    push(ag, (1, 1), 2)
    gap(2)
    push(ag, (1, 1), 3)
    push(ag, (1, 0), 5, mark=(1, 0))
    push(ag, (1, 1), 4)
    push(ag, (1, 2), 2)
    gap(2)
    gap(2)
    push(ag, (1, 2), 3)
    gap(10)
    push(ag, (1, 2), 4)
    push(ag, (1, 1), 5, mark=(1, 1))
    push(ag, (1, 2), 5, mark=(1, 2))

    @pl.loop(0, images)
    def _(i):
        rs_ = row_slice(i)
        out_ref[rs_, :] = x_ref[rs_, :].astype(F32)

    forward(0, out_ref)
    spill()
    permute(mid, out_ref, SHIFT)
    forward(1, mid)
    permute(out_ref, mid, GRID - SHIFT)

    @pl.loop(0, images)
    def _(i):
        rs_ = row_slice(i)
        gin_ref[rs_, :] = cot_ref[rs_, :].astype(F32)

    permute(mid, gin_ref, SHIFT)
    backward(1, mid)
    permute(gin_ref, mid, GRID - SHIFT)
    for copy in fetched:
        copy.wait()
    sent(gathers.values())
    backward(0, gin_ref)
    sm(0)
    tick(1)
    sm(1)
    tick(1)
    sm(2)
    tick(1)
    sm(3)
    tick(1)
    sm(4)
    tick(len(queue))
    for found in scatters.values():
        for _, _, groups in found:
            for group in groups:
                for copy in group:
                    copy.wait_send()
    for group in sums + [small_in]:
        for copy in group:
            copy.wait_send()


def fast_device(
    inputs, cotangent, region_ids, rel_index, norm1_gain, norm1_bias, w_qkv, qv_bias, bias_table, w_proj,
    proj_bias, norm2_gain, norm2_bias, w_fc1, fc1_bias, w_fc2, fc2_bias,
):
    t_index = lax.axis_index("tensor")
    tokens, width = inputs.shape
    plan = Plan(lax.axis_size("dp"), tokens, width, fc1_bias.shape[1], bias_table.shape[1])
    win_tokens = WIN * WIN
    pad = SLOT - win_tokens
    L, T, Z, local, ffl, hl = LAYERS, plan.T, plan.Z, plan.local, plan.ffl, plan.heads_local
    R, C, M = plan.shard, plan.cols, plan.rows

    def padded(array):
        spread_ = array.reshape(tokens // win_tokens, win_tokens, width)
        return jnp.pad(spread_, ((0, 0), (0, pad), (0, 0))).reshape(M, width)

    shards = jnp.stack([pack_weights(w_qkv[l], w_proj[l], w_fc1[l], w_fc2[l]) for l in range(L)])
    vec = jnp.zeros((L, 8, ffl), F32)
    vec = vec.at[:, 0].set(fc1_bias.astype(F32))
    vec = vec.at[:, 1:3, :local].set(qv_bias.astype(F32))
    tab = jnp.pad(bias_table.astype(F32), ((0, 0), (0, 0), (0, TABLE_LANES - TABLE)))
    params = jnp.stack([norm1_gain, norm1_bias, proj_bias, norm2_gain, norm2_bias, fc2_bias], axis=1).astype(F32)
    params = jnp.pad(params, ((0, 0), (0, 2), (0, 0)))
    index_padded = jnp.pad(rel_index.T, ((0, pad), (0, pad)), constant_values=-1)
    hot = (index_padded[:, :, None] == jnp.arange(TABLE_LANES, dtype=jnp.int32)).astype(BF16)
    regions = region_ids.reshape(plan.windows, win_tokens)
    shift_mask = jnp.where(regions[:, :, None] == regions[:, None, :], 0.0, MASKED).astype(F32)
    mask = jnp.concatenate([jnp.zeros_like(shift_mask[:1]), shift_mask], axis=0)
    mask = jnp.pad(mask, ((0, 0), (0, 0), (0, pad)))
    mask = jnp.pad(mask, ((0, 0), (0, pad), (0, 0)), constant_values=PADDED)
    mask = jnp.tile(mask, (1, 1, PACK))

    vmem = pl.BlockSpec(memory_space=pltpu.VMEM)
    anywhere = pl.BlockSpec(memory_space=pl.ANY)
    n_ag, n_rs = L * 3 * 2, L * 4 * 2
    DMA = pltpu.SemaphoreType.DMA
    outs = pl.pallas_call(
        functools.partial(step_kernel, plan),
        out_shape=(
            jax.ShapeDtypeStruct((M, width), F32),
            jax.ShapeDtypeStruct((M, width), F32),
            jax.ShapeDtypeStruct((L, R, C), F32),
            jax.ShapeDtypeStruct((L, SMALL_ROWS, width), F32),
            jax.ShapeDtypeStruct((2, M, T * ffl), BF16),
            jax.ShapeDtypeStruct((5, M, width), BF16),
            jax.ShapeDtypeStruct((2, M, 1), F32),
            jax.ShapeDtypeStruct((M, 3 * width), BF16),
        ),
        in_specs=[vmem] * 8,
        out_specs=(vmem,) * 4 + (anywhere,) * 4,
        scratch_shapes=[
            pltpu.VMEM((L, T, Z, 2, 2, R, C), BF16),
            pltpu.VMEM((T, Z, 2, 2, R, C), BF16),
            pltpu.VMEM((T, L, 8, ffl), F32),
            pltpu.VMEM((T, L, hl, TABLE_LANES), F32),
            pltpu.VMEM((2, M, T * ffl), BF16),
            pltpu.VMEM((5, M, width), BF16),
            pltpu.VMEM((2, M, 1), F32),
            pltpu.VMEM((M, 3 * width), BF16),
            pltpu.VMEM((M, width), BF16),
            pltpu.VMEM((M, width), F32),
            pltpu.VMEM(((plan.windows + 1) * plan.groups, SLOT, PACK * SLOT), F32),
            pltpu.VMEM((8, SLOT, PACK * SLOT), F32),
            pltpu.VMEM((2, 8, width), F32),
            pltpu.VMEM((L, SMALL_ROWS, width), F32),
            pltpu.VMEM((4, L, SMALL_ROWS, width), F32),
            pltpu.VMEM((L, Z, 2, 2, R, C), BF16),
            pltpu.VMEM((L, Z, 2, R, C), BF16),
            pltpu.VMEM((L, Z, R, C), BF16),
            pltpu.VMEM((L, Z - 1, R, C), BF16),
            pltpu.VMEM((Z + 2, L, SMALL_ROWS, width), F32),
            DMA((n_ag, Z + 4)),
            DMA((n_ag, Z + 4)),
            DMA((n_rs, Z + 2)),
            DMA((n_rs, Z + 2)),
            DMA((Z + 4,)),
            DMA((Z + 4,)),
            DMA((8,)),
        ],
        compiler_params=pltpu.CompilerParams(
            collective_id=0, has_side_effects=True, vmem_limit_bytes=67043328
        ),
        name="whole_step",
    )(padded(inputs), padded(cotangent), shards, vec, tab, params, mask, hot)
    out, g_in, grads, total = outs[:4]

    def unpadded(array):
        return array.reshape(-1, SLOT, width)[:, :win_tokens].reshape(tokens, width)

    qv_total = lax.dynamic_slice_in_dim(total[:, 6:8], t_index * local, local, 2)
    fc1_total = total[:, 8 : 8 + T * ffl // width].reshape(L, T * ffl)
    fc1_total = lax.dynamic_slice_in_dim(fc1_total, t_index * ffl, ffl, 1)
    table_total = total[:, 16 : 16 + 2 * plan.groups].reshape(L, 2, plan.groups, PACK // 2, TABLE_LANES)
    table_total = table_total.transpose(0, 2, 3, 1, 4).reshape(L, T * hl, TABLE_LANES)
    table_total = lax.dynamic_slice_in_dim(table_total, t_index * hl, hl, 1)[..., :TABLE]
    a, b, c = 3 * local, 4 * local, 4 * local + ffl
    return (
        unpadded(out), unpadded(g_in), total[:, 0], total[:, 1],
        grads[..., :a].reshape(L, R, 3, local).transpose(0, 2, 1, 3),
        qv_total, table_total,
        grads[..., a:b].transpose(0, 2, 1),
        total[:, 2], total[:, 3], total[:, 4],
        grads[..., b:c], fc1_total,
        grads[..., c:].transpose(0, 2, 1),
        total[:, 5],
    )


def one_kernel_fits(inputs, bias_table, fc1_bias):
    n_dp, n_t = lax.axis_size("dp"), lax.axis_size("tensor")
    tokens, width = inputs.shape
    z = n_dp // 4
    heads_local = bias_table.shape[1]
    return (
        n_t == 2 and n_dp % 4 == 0 and z >= 2 and z & (z - 1) == 0
        and heads_local * HD % LANES == 0 and heads_local == 2 * LANES // HD and LAYERS == 2
        and width // n_dp % 16 == 0 and width == 2 * TABLE_LANES and fc1_bias.shape[1] % width == 0
        and 8 + 2 * fc1_bias.shape[1] // width <= 16
        and tokens % (GRID * GRID) == 0 and tokens <= 4 * GRID * GRID
    )


def choose(*args):
    if one_kernel_fits(args[0], args[8], args[14]):
        return fast_device(*args)
    return per_device(*args)


def solution(mesh):
    in_specs = (
        P(("dp", "tensor"), None),
        P(("dp", "tensor"), None),
        P(),
        P(),
        P(),
        P(),
        P(None, None, "dp", "tensor"),
        P(None, None, "tensor"),
        P(None, "tensor", None),
        P(None, "tensor", "dp"),
        P(),
        P(),
        P(),
        P(None, "dp", "tensor"),
        P(None, "tensor"),
        P(None, "tensor", "dp"),
        P(),
    )
    out_specs = (
        P(("dp", "tensor"), None),
        P(("dp", "tensor"), None),
        P(),
        P(),
        P(None, None, "dp", "tensor"),
        P(None, None, "tensor"),
        P(None, "tensor", None),
        P(None, "tensor", "dp"),
        P(),
        P(),
        P(),
        P(None, "dp", "tensor"),
        P(None, "tensor"),
        P(None, "tensor", "dp"),
        P(),
    )
    return jax.shard_map(
        choose, mesh=mesh, in_specs=in_specs, out_specs=out_specs, check_vma=False
    )
```
